32 devices in a mesh: section: 4 (over z), dom: 4 (over y, x), ens: 2 (over core).
Axes of the slice: x: 2, y: 2, z: 4, core: 2. Of those that a mesh axis runs over, the one named last changes fastest.
Arguments:
- members: bfloat16 [8, 512, 512], P(('section', 'ens'), 'dom'), may hold values from -6 to 6
- layer_mats: bfloat16 [4, 6, 512, 512], P('section'), may hold values from -0.25 to 0.25
- biases: float32 [4, 2, 512], P('section'), may hold values from -3 to 3
- norm_gains: float32 [4, 2, 512], P('section'), may hold values from 0.25 to 1.75
- edge_blocks: int32 [4, 6], P('dom'), may hold values from 0 to 2
- edge_shift: int32 [4, 6], P('dom'), may hold values from 0 to 127
Outputs:
- final_state: bfloat16 [8, 512, 512], P(('section', 'ens'), 'dom')
- ens_mean: float32 [512, 512], P('dom')
The draws below stay inside these ranges and needn't reach their ends.
Inputs may be any that keep to these rules, and one draw needn't show every extreme that they name: `edge_blocks`: a frame of 1 block of the previous part (wrapping around), the part's own 1 block, then 1 block of the next part.
All inputs are finite; a program needn't handle non-finite values.
Results may differ from the reference program's by a relative error of at most 0.022.
Values may be sent and summed in bfloat16 or wider, within the bound.
No kernel may reach another device: no remote copies, remote signals or barrier semaphores. Data moves between devices by JAX's collectives and lax.ppermute only.
A program may use at most 64 MiB of HBM per device.

```python
import jax
import jax.numpy as jnp
from jax import lax

D = 512
BLK = 128
HB = 1
SLOTS = 6
BD = 1
NODES = 512
NBLK = 4
MEMBERS = 8
LAYERS = 4


def touch_ends(entries, stream_key, low, top_value):
    spot = [jax.random.randint(jax.random.fold_in(stream_key, axis), (), 0, length) for axis, length in enumerate(entries.shape)]
    widest = entries.shape.index(max(entries.shape))
    beside = spot[:widest] + [(spot[widest] + 1) % entries.shape[widest]] + spot[widest + 1:]
    return entries.at[tuple(spot)].set(low).at[tuple(beside)].set(top_value)


def shard_levels(stream_key, shape, cuts, least, high):
    factor_of = 1.0
    for axis_at, parts in cuts:
        steps = jax.random.uniform(jax.random.fold_in(jax.random.fold_in(stream_key, 6), axis_at), (parts,), jnp.float32, least / len(cuts), high / len(cuts))
        factor_of = factor_of * jnp.repeat(jnp.exp(steps), shape[axis_at] // parts).reshape((-1,) + (1,) * (len(shape) - 1 - axis_at))
    return factor_of


def scatter_about(own_key, dims, deviation, bound, shards=(), kind=jnp.bfloat16):
    entries = deviation * jax.random.normal(own_key, dims, jnp.float32)
    if shards:
        entries = entries * shard_levels(own_key, dims, shards, -0.22, 0.18)
    return jnp.clip(entries, -bound, bound).astype(kind)


def setup_inputs(seed: int = 0) -> dict:
    seeds = jax.random.split(jax.random.key(seed), 7)
    return {
        "members": scatter_about(seeds[0], (MEMBERS, NODES, D), 1.0, 6.0, ((0, 8), (1, 4))),
        "layer_mats": scatter_about(seeds[1], (LAYERS, 6, D, D), D ** -0.5, 0.25, ((0, 4),)),
        "biases": scatter_about(seeds[2], (LAYERS, 2, D), 0.5, 3.0, ((0, 4),), jnp.float32),
        "norm_gains": jnp.clip(1.0 + 0.15 * jax.random.normal(seeds[3], (LAYERS, 2, D), jnp.float32), 0.25, 1.75),
        "edge_blocks": touch_ends(jax.random.randint(seeds[4], (NBLK, SLOTS), 0, BD + 2 * HB), jax.random.fold_in(seeds[4], 1), 0, (BD + 2 * HB) - 1).astype(jnp.int32),
        "edge_shift": touch_ends(jax.random.randint(seeds[5], (NBLK, SLOTS), 0, BLK), jax.random.fold_in(seeds[5], 1), 0, BLK - 1).astype(jnp.int32),
    }


EPSILON = 1e-05

def layer_norm(values):
    average = lax.optimization_barrier(jnp.mean(values, axis=-1, keepdims=True))
    centred = values - average
    spread = lax.optimization_barrier(jnp.mean(centred * centred, axis=-1, keepdims=True))
    return centred * lax.rsqrt(spread + EPSILON)

def node_update(state, sender_terms, sender_rows, matrices, bias_pair, gain_pair):
    width_d = state.shape[-1]
    receiver_terms = jnp.dot(state, matrices[1], preferred_element_type=jnp.float32) + bias_pair[0]
    picked = jnp.take(sender_terms, sender_rows.reshape(-1), axis=0).reshape(sender_rows.shape + (width_d,))
    pre_act = picked.astype(jnp.float32) + receiver_terms[:, None, :]
    hidden = jax.nn.silu(pre_act).astype(jnp.bfloat16)
    edge_out = jnp.dot(hidden.reshape(-1, width_d), matrices[2], preferred_element_type=jnp.float32)
    edge_out = edge_out.reshape(hidden.shape)
    messages = lax.optimization_barrier(jnp.sum(layer_norm(edge_out) * gain_pair[0], axis=1)).astype(jnp.bfloat16)
    node_pre = jnp.dot(state, matrices[3], preferred_element_type=jnp.float32) + jnp.dot(messages, matrices[4], preferred_element_type=jnp.float32) + bias_pair[1]
    node_hidden = jax.nn.silu(node_pre).astype(jnp.bfloat16)
    node_out = jnp.dot(node_hidden, matrices[5], preferred_element_type=jnp.float32)
    return (state.astype(jnp.float32) + layer_norm(node_out) * gain_pair[1]).astype(jnp.bfloat16)

def reference(members, layer_mats, biases, norm_gains, edge_blocks, edge_shift):
    node_ids = jnp.arange(NODES, dtype=jnp.int32)
    block_ids = node_ids // BLK
    positions = node_ids % BLK
    owners = block_ids // BD
    frame_block = edge_blocks[block_ids]
    offsets = edge_shift[block_ids]
    global_block = (owners[:, None] * BD + frame_block - HB) % NBLK
    sender_rows = (global_block * BLK + (positions[:, None] + offsets) % BLK).astype(jnp.int32)

    def rollout(state):
        for layer_no in range(LAYERS):
            matrices = layer_mats[layer_no]
            sender_terms = jnp.dot(state, matrices[0], preferred_element_type=jnp.float32).astype(jnp.bfloat16)
            state = node_update(state, sender_terms, sender_rows, matrices, biases[layer_no], norm_gains[layer_no])
        return state
    final_state = lax.map(rollout, members)
    ens_mean = lax.optimization_barrier(jnp.sum(final_state.astype(jnp.float32), axis=0)) / MEMBERS
    return (final_state, ens_mean)
```

```python
import functools

import jax
import jax.numpy as jnp
from jax import lax
from jax.experimental import pallas as pl
from jax.experimental.pallas import tpu as pltpu
from jax.sharding import PartitionSpec as P

BLK = 128
HB = 1
EPSILON = 1e-05
MATS = 6
F32 = jnp.float32
BF16 = jnp.bfloat16
AXES = ("section", "dom", "ens")
HOME = 1


def with_halo(x, sides, width):
    for axis, dim in sides:
        devices, length = (lax.axis_size(axis), x.shape[dim])
        up = [(i, (i + 1) % devices) for i in range(devices)]
        down = [(j, i) for i, j in up]
        last = lax.slice_in_dim(x, length - width, length, axis=dim)
        first = lax.slice_in_dim(x, 0, width, axis=dim)
        before = lax.ppermute(last, axis, up)
        after = lax.ppermute(first, axis, down)
        x = jnp.concatenate([before, x, after], axis=dim)
    return x


def from_behind(x, axis, by):
    devices = lax.axis_size(axis)
    return lax.ppermute(x, axis, [(i, (i + by) % devices) for i in range(devices)])


def layer_norm(values):
    average = jnp.mean(values, axis=-1, keepdims=True)
    centred = values - average
    spread = jnp.mean(centred * centred, axis=-1, keepdims=True)
    return centred * lax.rsqrt(spread + EPSILON)


def project(values, weight):
    return jnp.einsum("mnd,de->mne", values, weight, preferred_element_type=jnp.float32)


def fetch_rim(state, send_weight):
    outgoing = project(state, send_weight).astype(jnp.bfloat16)
    extended = with_halo(outgoing, (("dom", 1),), HB * BLK)
    return extended


def update_nodes(state, sender_terms, sender_rows, matrices, bias_pair, gain_pair):
    batch_size, node_count, width_d = state.shape
    slot_count = sender_rows.shape[1]
    receiver_terms = project(state, matrices[1]) + bias_pair[0]
    picked = jnp.take(sender_terms, sender_rows.reshape(-1), axis=1).reshape(
        batch_size, node_count, slot_count, width_d
    )
    pre_act = picked.astype(jnp.float32) + receiver_terms[:, :, None, :]
    hidden = jax.nn.silu(pre_act).astype(jnp.bfloat16)
    edge_out = jnp.einsum("mnkd,de->mnke", hidden, matrices[2], preferred_element_type=jnp.float32)
    messages = jnp.sum(layer_norm(edge_out) * gain_pair[0], axis=2).astype(jnp.bfloat16)
    node_pre = project(state, matrices[3]) + project(messages, matrices[4]) + bias_pair[1]
    node_hidden = jax.nn.silu(node_pre).astype(jnp.bfloat16)
    node_out = project(node_hidden, matrices[5])
    return (state.astype(jnp.float32) + layer_norm(node_out) * gain_pair[1]).astype(jnp.bfloat16)


def in_rounds(members, layer_mats, biases, norm_gains, edge_blocks, edge_shift):
    blocks = edge_blocks.shape[0]
    block_rows = jnp.repeat(edge_blocks, BLK, axis=0)
    row_offsets = jnp.repeat(edge_shift, BLK, axis=0)
    positions = (jnp.arange(blocks * BLK, dtype=jnp.int32) % BLK)[:, None]
    sender_rows = block_rows * BLK + (positions + row_offsets) % BLK
    sections = lax.axis_size("section")
    section_index = lax.axis_index("section")
    matrices = layer_mats[0]
    bias_pair = biases[0]
    gain_pair = norm_gains[0]

    def advance(moment, state):
        anchor = (section_index - moment) % sections
        entry_tick = (sections - anchor) % sections
        active = jnp.logical_and(moment >= entry_tick, moment - entry_tick < sections)
        sender_terms = fetch_rim(state, matrices[0])
        state = lax.cond(
            active,
            lambda: update_nodes(state, sender_terms, sender_rows, matrices, bias_pair, gain_pair),
            lambda: state,
        )
        return from_behind(state, "section", 1)

    final_state = lax.fori_loop(0, 2 * sections, advance, members)
    member_count = final_state.shape[0] * sections * lax.axis_size("ens")
    member_total = lax.psum(
        jnp.sum(final_state.astype(jnp.float32), axis=0).astype(jnp.bfloat16), ("section", "ens")
    ).astype(jnp.float32)
    return (final_state, member_total / member_count)


def silu(v):
    half = 0.5 * v
    return half + half * jnp.tanh(half)


def norm(v):
    scale = 1.0 / v.shape[-1]
    centred = v - jnp.sum(v, axis=-1, keepdims=True) * scale
    spread = jnp.sum(centred * centred, axis=-1, keepdims=True) * scale
    return centred * lax.rsqrt(spread + EPSILON)


def dot(a, b):
    return jnp.dot(a, b, preferred_element_type=F32)


def shifted_block(senders, block, shift):
    width = senders.shape[2]
    base = pl.multiple_of((shift // 8) * 8, 8)
    rest = shift % 8
    rows = senders[block, pl.ds(base, BLK + 8), :].reshape(BLK // 8 + 1, 8, width)
    turned = pltpu.roll(rows, (8 - rest) % 8, 1)
    place = lax.broadcasted_iota(jnp.int32, (1, 8, width), 1)
    return jnp.where(place < 8 - rest, turned[:-1], turned[1:]).reshape(BLK, width)


def layer_kernel(parts, first, last, slots, *refs):
    starts, table, state = refs[:3]
    refs = refs[3:]
    if first == 3:
        given, refs = refs[0], refs[1:]
    pieces, refs = refs[: len(parts)], refs[len(parts) :]
    terms, out, mats = refs[:3]
    width = state.shape[1]
    blocks = state.shape[0] // BLK
    copies = []
    sems = refs[-1]
    for i, rows in enumerate(parts):
        at = pl.multiple_of(starts[i], BLK)
        copies.append(pltpu.make_async_copy(pieces[i], mats.at[pl.ds(at, rows), :], sems.at[i]))
    for copy in copies:
        copy.start()
    for copy in copies:
        copy.wait()

    def mat(i):
        return mats[(i - first) * width : (i - first + 1) * width, :]

    if first == 0:
        senders, hidden = refs[3], refs[4]
        sent = dot(state[...], mat(0)).astype(BF16).astype(F32)
        for b in range(blocks):
            own = sent[b * BLK : (b + 1) * BLK]
            senders[b, 0:BLK] = own
            senders[b, BLK : 2 * BLK] = own
        received = dot(state[...], mat(1)) + terms[0:1]
        collected = []
        for b in range(blocks):
            for k in range(slots):
                block = table[b * 2 * slots + k]
                shift = table[b * 2 * slots + slots + k]
                v = shifted_block(senders, block, shift) + received[b * BLK : (b + 1) * BLK]
                hidden[b, k * BLK : (k + 1) * BLK] = silu(v).astype(BF16)
            e = dot(hidden[b], mat(2))
            total = norm(e[0:BLK])
            for k in range(1, slots):
                total += norm(e[k * BLK : (k + 1) * BLK])
            collected.append((total * terms[2:3]).astype(BF16))
        messages = jnp.concatenate(collected, axis=0)
        if last == 3:
            out[...] = messages
            return
    else:
        messages = given[...]
    pre = dot(state[...], mat(3)) + dot(messages, mat(4)) + terms[1:2]
    node_out = dot(silu(pre).astype(BF16), mat(5))
    out[...] = (state[...].astype(F32) + norm(node_out) * terms[3:4]).astype(BF16)


def run_layer(state, table, slots, terms, parts, first=0, last=MATS, messages=None):
    rows, width = state.shape
    blocks = rows // BLK
    pieces = [p for p, _ in parts]
    starts = jnp.stack([jnp.asarray(at, jnp.int32) for _, at in parts])
    sizes = tuple(p.shape[0] for p in pieces)
    smem = pl.BlockSpec(memory_space=pltpu.SMEM)
    vmem = pl.BlockSpec(memory_space=pltpu.VMEM)
    scratch = [pltpu.VMEM(((last - first) * width, width), BF16)]
    if first == 0:
        scratch += [
            pltpu.VMEM((blocks, 2 * BLK + 8, width), F32),
            pltpu.VMEM((blocks, slots * BLK, width), BF16),
        ]
    scratch.append(pltpu.SemaphoreType.DMA((len(pieces),)))
    given = [] if messages is None else [messages]
    edge = 2 * rows * slots * width * width if first == 0 else 0
    flops = edge + 2 * rows * width * width * 2 * (1 if last - first == 3 else 2)
    return pl.pallas_call(
        functools.partial(layer_kernel, sizes, first, last, slots),
        out_shape=jax.ShapeDtypeStruct((rows, width), BF16),
        in_specs=[smem, smem, vmem]
        + [vmem] * len(given)
        + [pl.BlockSpec(memory_space=pl.ANY)] * len(pieces)
        + [vmem],
        out_specs=vmem,
        scratch_shapes=scratch,
        cost_estimate=pl.CostEstimate(
            flops=flops, bytes_accessed=2 * (last - first) * width * width, transcendentals=rows * slots * width
        ),
        compiler_params=pltpu.CompilerParams(vmem_limit_bytes=40 << 20),
    )(starts, table, state, *given, *pieces, terms)


def on_plane(members, layer_mats, biases, norm_gains, edge_blocks, edge_shift):
    doms, cores = lax.axis_size("dom"), lax.axis_size("ens")
    layers = lax.axis_size("section")
    s, d, e = (lax.axis_index(a) for a in AXES)
    slots = edge_blocks.shape[1]
    width = members.shape[2]
    mats = layer_mats[0].reshape(MATS * width, width)
    half, quarter, eighth = (MATS * width // n for n in (2, 4, 8))

    def index(i, j, k):
        return (i * doms + j) * cores + k

    def send(x, pairs):
        return lax.ppermute(x, AXES, [(index(*a), index(*b)) for a, b in pairs])

    chips = [(j, k) for j in range(doms) for k in range(cores)]
    spots = [(i, j, k) for i in range(layers) for j, k in chips]

    def up(x, *hops):
        return send(x, [((i, j, k), (t, j, k)) for i, t in hops for j, k in chips])

    def across(x, by):
        return send(x, [((HOME, j, k), (HOME, j ^ by, k)) for j, k in chips])

    def partner(x):
        return send(x, [((HOME, j, k), (HOME, j, 1 - k)) for j, k in chips])

    def own_rows(start, rows):
        return lax.dynamic_slice_in_dim(mats, start, rows, axis=0)

    parity = (d & 1) ^ (d >> 1)
    mine = quarter * e
    outer = own_rows(jnp.where(s == 0, 0, half * parity) + mine, quarter)
    first_half = up(outer, (0, HOME), (3, 2))
    two_half = up(own_rows(half * parity + mine, quarter), (2, HOME))
    second_half = up(own_rows(half + mine, quarter), (0, HOME))
    three_half = up(first_half, (2, HOME))

    lists = jnp.concatenate([edge_blocks[0], edge_shift[0]]).astype(BF16)
    tail = jnp.zeros((16, width), BF16).at[0, : 2 * slots].set(lists)
    parcel = jnp.concatenate([members[0], tail], axis=0)
    arrived = [
        send(parcel, [((i, i ^ r, k), (HOME, i, k)) for i in range(layers) for k in range(cores)])
        for r in range(doms)
    ]
    state = jnp.concatenate([a[:BLK] for a in arrived], axis=0)
    lists = jnp.stack([a[BLK, : 2 * slots] for a in arrived]).astype(jnp.int32)
    block_of = d ^ jnp.arange(doms, dtype=jnp.int32)[:, None]
    sender_slot = ((block_of + lists[:, :slots] + (doms - HB)) % doms) ^ d
    table = jnp.concatenate([sender_slot, lists[:, slots:]], axis=1).reshape(-1)

    terms = jnp.concatenate([biases[0], norm_gains[0]], axis=0)
    terms0, terms2, terms3 = (up(terms, (i, HOME)) for i in (0, 2, 3))

    def pair_up(x, start):
        return [(x, start + mine), (partner(x), start + quarter - mine)]

    def spread(x):
        near = across(x[:eighth], 1)
        far = across(x[eighth:], 2)
        base, other = half * parity, half - half * parity
        parts = []
        for piece, at in ((x, base), (near, other), (far, other + eighth)):
            parts += [(piece, at + mine), (partner(piece), at + quarter - mine)]
        return parts

    early = pair_up(first_half, 0)
    late = pair_up(second_half, 0)
    messages = run_layer(state, table, slots, terms0, early, 0, 3)
    state = run_layer(state, table, slots, terms0, late, 3, MATS, messages)
    state = run_layer(state, table, slots, terms, [(mats, 0)])
    state = run_layer(state, table, slots, terms2, spread(two_half))
    state = run_layer(state, table, slots, terms3, spread(three_half))

    blocks = [state[r * BLK : (r + 1) * BLK] for r in range(doms)]
    columns = [blocks[0]] + [across(blocks[r], r) for r in range(1, doms)]
    part = sum(c.astype(F32) for c in columns).astype(BF16)
    total = (part.astype(F32) + partner(part).astype(F32)).astype(BF16)
    returned = [
        send(columns[r], [((HOME, j, k), (j ^ r, j, k)) for j, k in chips]) for r in range(doms)
    ]
    final = returned[0]
    for r in range(1, doms):
        final = jnp.where(s == d ^ r, returned[r], final)
    sums = total
    for i in range(layers):
        if i != HOME:
            sums = jnp.where(s == i, up(total, (HOME, i)), sums)
    count = members.shape[0] * layers * cores
    return (final[None], sums.astype(F32) / count)


def solution(mesh):
    shape = dict(mesh.shape)
    placed = (
        P(("section", "ens"), "dom", None),
        P("section", None, None, None),
        P("section", None, None),
        P("section", None, None),
        P("dom", None),
        P("dom", None),
    )

    def on_device(members, layer_mats, biases, norm_gains, edge_blocks, edge_shift):
        small = shape["section"] == 4 and shape["dom"] == 4 and shape["ens"] == 2
        one_each = members.shape[:2] == (1, BLK) and layer_mats.shape[0] == 1
        plan = on_plane if small and one_each else in_rounds
        return plan(members, layer_mats, biases, norm_gains, edge_blocks, edge_shift)

    return jax.shard_map(
        on_device,
        mesh=mesh,
        in_specs=placed,
        out_specs=(P(("section", "ens"), "dom", None), P("dom", None)),
        check_vma=False,
    )
```

```python
import functools

import jax
import jax.numpy as jnp
from jax import lax
from jax.experimental import pallas as pl
from jax.experimental.pallas import tpu as pltpu
from jax.sharding import PartitionSpec as P

BLK = 128
HB = 1
EPSILON = 1e-05
MATS = 6
F32 = jnp.float32
BF16 = jnp.bfloat16
AXES = ("section", "dom", "ens")
HOME = 1


def with_halo(x, sides, width):
    for axis, dim in sides:
        devices, length = (lax.axis_size(axis), x.shape[dim])
        up = [(i, (i + 1) % devices) for i in range(devices)]
        down = [(j, i) for i, j in up]
        last = lax.slice_in_dim(x, length - width, length, axis=dim)
        first = lax.slice_in_dim(x, 0, width, axis=dim)
        before = lax.ppermute(last, axis, up)
        after = lax.ppermute(first, axis, down)
        x = jnp.concatenate([before, x, after], axis=dim)
    return x


def from_behind(x, axis, by):
    devices = lax.axis_size(axis)
    return lax.ppermute(x, axis, [(i, (i + by) % devices) for i in range(devices)])


def layer_norm(values):
    average = jnp.mean(values, axis=-1, keepdims=True)
    centred = values - average
    spread = jnp.mean(centred * centred, axis=-1, keepdims=True)
    return centred * lax.rsqrt(spread + EPSILON)


def project(values, weight):
    return jnp.einsum("mnd,de->mne", values, weight, preferred_element_type=jnp.float32)


def fetch_rim(state, send_weight):
    outgoing = project(state, send_weight).astype(jnp.bfloat16)
    extended = with_halo(outgoing, (("dom", 1),), HB * BLK)
    return extended


def update_nodes(state, sender_terms, sender_rows, matrices, bias_pair, gain_pair):
    batch_size, node_count, width_d = state.shape
    slot_count = sender_rows.shape[1]
    receiver_terms = project(state, matrices[1]) + bias_pair[0]
    picked = jnp.take(sender_terms, sender_rows.reshape(-1), axis=1).reshape(
        batch_size, node_count, slot_count, width_d
    )
    pre_act = picked.astype(jnp.float32) + receiver_terms[:, :, None, :]
    hidden = jax.nn.silu(pre_act).astype(jnp.bfloat16)
    edge_out = jnp.einsum("mnkd,de->mnke", hidden, matrices[2], preferred_element_type=jnp.float32)
    messages = jnp.sum(layer_norm(edge_out) * gain_pair[0], axis=2).astype(jnp.bfloat16)
    node_pre = project(state, matrices[3]) + project(messages, matrices[4]) + bias_pair[1]
    node_hidden = jax.nn.silu(node_pre).astype(jnp.bfloat16)
    node_out = project(node_hidden, matrices[5])
    return (state.astype(jnp.float32) + layer_norm(node_out) * gain_pair[1]).astype(jnp.bfloat16)


def in_rounds(members, layer_mats, biases, norm_gains, edge_blocks, edge_shift):
    blocks = edge_blocks.shape[0]
    block_rows = jnp.repeat(edge_blocks, BLK, axis=0)
    row_offsets = jnp.repeat(edge_shift, BLK, axis=0)
    positions = (jnp.arange(blocks * BLK, dtype=jnp.int32) % BLK)[:, None]
    sender_rows = block_rows * BLK + (positions + row_offsets) % BLK
    sections = lax.axis_size("section")
    section_index = lax.axis_index("section")
    matrices = layer_mats[0]
    bias_pair = biases[0]
    gain_pair = norm_gains[0]

    def advance(moment, state):
        anchor = (section_index - moment) % sections
        entry_tick = (sections - anchor) % sections
        active = jnp.logical_and(moment >= entry_tick, moment - entry_tick < sections)
        sender_terms = fetch_rim(state, matrices[0])
        state = lax.cond(
            active,
            lambda: update_nodes(state, sender_terms, sender_rows, matrices, bias_pair, gain_pair),
            lambda: state,
        )
        return from_behind(state, "section", 1)

    final_state = lax.fori_loop(0, 2 * sections, advance, members)
    member_count = final_state.shape[0] * sections * lax.axis_size("ens")
    member_total = lax.psum(
        jnp.sum(final_state.astype(jnp.float32), axis=0).astype(jnp.bfloat16), ("section", "ens")
    ).astype(jnp.float32)
    return (final_state, member_total / member_count)


def silu(v):
    half = 0.5 * v
    return half + half * jnp.tanh(half)


def norm(v):
    scale = 1.0 / v.shape[-1]
    centred = v - jnp.sum(v, axis=-1, keepdims=True) * scale
    spread = jnp.sum(centred * centred, axis=-1, keepdims=True) * scale
    return centred * lax.rsqrt(spread + EPSILON)


def dot(a, b):
    return jnp.dot(a, b, preferred_element_type=F32)


def shifted_block(senders, block, shift):
    width = senders.shape[2]
    base = pl.multiple_of((shift // 8) * 8, 8)
    rest = shift % 8
    rows = senders[block, pl.ds(base, BLK + 8), :].reshape(BLK // 8 + 1, 8, width)
    turned = pltpu.roll(rows, (8 - rest) % 8, 1)
    place = lax.broadcasted_iota(jnp.int32, (1, 8, width), 1)
    return jnp.where(place < 8 - rest, turned[:-1], turned[1:]).reshape(BLK, width)


def layer_kernel(cuts, slots, tail, *refs):
    starts, table, state, terms = refs[:4]
    refs = refs[4:]
    count = 1 + max(c[0] for c in cuts)
    pieces, refs = refs[:count], refs[count:]
    if tail:
        trailer, refs = refs[0], refs[1:]
    out, mats, senders, hidden, sems = refs
    width = state.shape[1]
    blocks = senders.shape[0]
    nodes = blocks * BLK
    copies = []
    for i, (piece, at, rows) in enumerate(cuts):
        to = pl.multiple_of(starts[i], BLK)
        copies.append(
            pltpu.make_async_copy(pieces[piece].at[pl.ds(at, rows), :], mats.at[pl.ds(to, rows), :], sems.at[i])
        )
    for copy in copies:
        copy.start()
    in_turn = len(cuts) == MATS
    if not in_turn:
        for copy in copies:
            copy.wait()

    def mat(i):
        if in_turn:
            copies[i].wait()
        return mats[i * width : (i + 1) * width, :]

    sent = dot(state[0:nodes], mat(0)).astype(BF16).astype(F32)
    for b in range(blocks):
        own = sent[b * BLK : (b + 1) * BLK]
        senders[b, 0:BLK] = own
        senders[b, BLK : 2 * BLK] = own
    received = dot(state[0:nodes], mat(1)) + terms[0:1]
    edge_mat = mat(2)
    collected = []
    for b in range(blocks):
        for k in range(slots):
            block = table[b * 2 * slots + k]
            shift = table[b * 2 * slots + slots + k]
            v = shifted_block(senders, block, shift) + received[b * BLK : (b + 1) * BLK]
            hidden[b, k * BLK : (k + 1) * BLK] = silu(v).astype(BF16)
        e = dot(hidden[b], edge_mat)
        total = norm(e[0:BLK])
        for k in range(1, slots):
            total += norm(e[k * BLK : (k + 1) * BLK])
        collected.append((total * terms[2:3]).astype(BF16))
    messages = jnp.concatenate(collected, axis=0)
    pre = dot(state[0:nodes], mat(3)) + dot(messages, mat(4)) + terms[1:2]
    node_out = dot(silu(pre).astype(BF16), mat(5))
    out[0:nodes] = (state[0:nodes].astype(F32) + norm(node_out) * terms[3:4]).astype(BF16)
    if tail:
        out[nodes:] = trailer[...]


def run_layer(state, table, slots, terms, pieces, cuts, starts, trailer=None):
    width = state.shape[1]
    blocks = state.shape[0] // BLK
    nodes = blocks * BLK
    tail = 0 if trailer is None else trailer.shape[0]
    smem = pl.BlockSpec(memory_space=pltpu.SMEM)
    vmem = pl.BlockSpec(memory_space=pltpu.VMEM)
    return pl.pallas_call(
        functools.partial(layer_kernel, cuts, slots, tail),
        out_shape=jax.ShapeDtypeStruct((nodes + tail, width), BF16),
        in_specs=[smem, smem, vmem, vmem]
        + [pl.BlockSpec(memory_space=pl.ANY)] * len(pieces)
        + [vmem] * (tail > 0),
        out_specs=vmem,
        scratch_shapes=[
            pltpu.VMEM((MATS * width, width), BF16),
            pltpu.VMEM((blocks, 2 * BLK + 8, width), F32),
            pltpu.VMEM((blocks, slots * BLK, width), BF16),
            pltpu.SemaphoreType.DMA((len(cuts),)),
        ],
        cost_estimate=pl.CostEstimate(
            flops=2 * nodes * (slots + 5) * width * width,
            bytes_accessed=2 * MATS * width * width,
            transcendentals=nodes * slots * width,
        ),
        compiler_params=pltpu.CompilerParams(vmem_limit_bytes=40 << 20),
    )(starts, table, state, terms, *pieces, *([trailer] if tail else []))


def gather_kernel(*refs):
    count = len(refs) // 2
    blocks, outs = refs[:count], refs[count:]
    total = blocks[0][...].astype(F32)
    for block in blocks[1:]:
        total += block[...].astype(F32)
    total = total.astype(BF16)
    rows = total.shape[0]
    for block, out in zip(blocks, outs):
        out[0:rows] = block[...]
        out[rows:] = total


def with_sum(blocks):
    rows, width = blocks[0].shape
    vmem = pl.BlockSpec(memory_space=pltpu.VMEM)
    return pl.pallas_call(
        gather_kernel,
        out_shape=[jax.ShapeDtypeStruct((2 * rows, width), BF16)] * len(blocks),
        in_specs=[vmem] * len(blocks),
        out_specs=[vmem] * len(blocks),
        cost_estimate=pl.CostEstimate(flops=len(blocks) * rows * width, bytes_accessed=0, transcendentals=0),
    )(*blocks)


def on_plane(members, layer_mats, biases, norm_gains, edge_blocks, edge_shift):
    doms, cores = lax.axis_size("dom"), lax.axis_size("ens")
    layers = lax.axis_size("section")
    s, d, e = (lax.axis_index(a) for a in AXES)
    slots = edge_blocks.shape[1]
    width = members.shape[2]
    mats = layer_mats[0].reshape(MATS * width, width)
    half, quarter, eighth = (MATS * width // n for n in (2, 4, 8))

    def index(i, j, k):
        return (i * doms + j) * cores + k

    def send(x, pairs):
        return lax.ppermute(x, AXES, [(index(*a), index(*b)) for a, b in pairs])

    chips = [(j, k) for j in range(doms) for k in range(cores)]

    def up(x, *hops):
        return send(x, [((i, j, k), (t, j, k)) for i, t in hops for j, k in chips])

    def across(x, by):
        return send(x, [((HOME, j, k), (HOME, j ^ by, k)) for j, k in chips])

    def partner(x, where=(HOME,)):
        return send(x, [((i, j, k), (i, j, 1 - k)) for i in where for j, k in chips])

    lists = jnp.concatenate([edge_blocks[0], edge_shift[0]]).astype(BF16)
    tail = jnp.zeros((16, width), BF16).at[0, : 2 * slots].set(lists)
    parcel = jnp.concatenate([members[0], tail], axis=0)
    arrived = [
        send(parcel, [((i, i ^ r, k), (0, i, k)) for i in range(layers) for k in range(cores)])
        for r in range(doms)
    ]
    state = jnp.concatenate([a[:BLK] for a in arrived], axis=0)
    trailer = jnp.concatenate([a[BLK : BLK + 4] for a in arrived], axis=0)

    def table_of(rows):
        lists = rows[:: 16 // doms, : 2 * slots].astype(jnp.int32)
        block_of = d ^ jnp.arange(doms, dtype=jnp.int32)[:, None]
        sender_slot = ((block_of + lists[:, :slots] + (doms - HB)) % doms) ^ d
        return jnp.concatenate([sender_slot, lists[:, slots:]], axis=1).reshape(-1)

    terms = jnp.concatenate([biases[0], norm_gains[0]], axis=0)
    addends, rest = [], terms
    for _ in range(3):
        head = lax.reduce_precision(rest, 8, 7)
        addends.append(head.astype(BF16))
        rest = rest - head
    riders = jnp.concatenate(addends + [jnp.zeros((4, width), BF16)], axis=0)
    parity = (d & 1) ^ (d >> 1)
    mine, other = half * parity, half - half * parity
    core, mate = quarter * e, quarter - quarter * e
    load = jnp.concatenate([lax.dynamic_slice_in_dim(mats, mine + core, quarter, axis=0), riders], axis=0)
    two = up(load, (2, HOME), (3, 2))
    three = up(two, (2, HOME))

    whole_cuts = tuple((0, i * width, width) for i in range(MATS))
    whole_starts = jnp.arange(MATS, dtype=jnp.int32) * width

    def spread(x):
        near = across(x[:eighth], 1)
        far = across(x[eighth:quarter], 2)
        pooled = jnp.concatenate([x[:quarter], near, far], axis=0)
        pieces = [pooled, partner(pooled)]
        cuts = tuple((p, at, rows) for p in (0, 1) for at, rows in ((0, quarter), (quarter, quarter)))
        starts = jnp.stack([mine + core, other + core, mine + mate, other + mate]).astype(jnp.int32)
        riding = x[quarter : quarter + 12].astype(F32)
        return riding[0:4] + riding[4:8] + riding[8:12], pieces, cuts, starts

    state = run_layer(state, table_of(trailer), slots, terms, [mats], whole_cuts, whole_starts, trailer)
    state = up(state, (0, HOME))
    table = table_of(state[doms * BLK :])
    state = run_layer(state, table, slots, terms, [mats], whole_cuts, whole_starts)
    state = run_layer(state, table, slots, *spread(two))
    state = run_layer(state, table, slots, *spread(three))

    blocks = [state[r * BLK : (r + 1) * BLK] for r in range(doms)]
    columns = with_sum([blocks[0]] + [across(blocks[r], r) for r in range(1, doms)])
    returned = [
        send(columns[r], [((HOME, j, k), (j ^ r, j, k)) for j, k in chips]) for r in range(doms)
    ]
    final = returned[0]
    for r in range(1, doms):
        final = jnp.where(s == d ^ r, returned[r], final)
    part = final[BLK:]
    total = part.astype(F32) + partner(part, range(layers)).astype(F32)
    count = members.shape[0] * layers * cores
    return (final[None, :BLK], total / count)


def solution(mesh):
    shape = dict(mesh.shape)
    placed = (
        P(("section", "ens"), "dom", None),
        P("section", None, None, None),
        P("section", None, None),
        P("section", None, None),
        P("dom", None),
        P("dom", None),
    )

    def on_device(members, layer_mats, biases, norm_gains, edge_blocks, edge_shift):
        small = shape["section"] == 4 and shape["dom"] == 4 and shape["ens"] == 2
        one_each = members.shape[:2] == (1, BLK) and layer_mats.shape[0] == 1
        plan = on_plane if small and one_each else in_rounds
        return plan(members, layer_mats, biases, norm_gains, edge_blocks, edge_shift)

    return jax.shard_map(
        on_device,
        mesh=mesh,
        in_specs=placed,
        out_specs=(P(("section", "ens"), "dom", None), P("dom", None)),
        check_vma=False,
    )
```

```python
import functools

import jax
import jax.numpy as jnp
from jax import lax
from jax.experimental import pallas as pl
from jax.experimental.pallas import tpu as pltpu
from jax.sharding import PartitionSpec as P

BLK = 128
HB = 1
EPSILON = 1e-05
MATS = 6
F32 = jnp.float32
BF16 = jnp.bfloat16
AXES = ("section", "dom", "ens")


def with_halo(x, sides, width):
    for axis, dim in sides:
        devices, length = (lax.axis_size(axis), x.shape[dim])
        up = [(i, (i + 1) % devices) for i in range(devices)]
        down = [(j, i) for i, j in up]
        last = lax.slice_in_dim(x, length - width, length, axis=dim)
        first = lax.slice_in_dim(x, 0, width, axis=dim)
        before = lax.ppermute(last, axis, up)
        after = lax.ppermute(first, axis, down)
        x = jnp.concatenate([before, x, after], axis=dim)
    return x


def from_behind(x, axis, by):
    devices = lax.axis_size(axis)
    return lax.ppermute(x, axis, [(i, (i + by) % devices) for i in range(devices)])


def layer_norm(values):
    average = jnp.mean(values, axis=-1, keepdims=True)
    centred = values - average
    spread = jnp.mean(centred * centred, axis=-1, keepdims=True)
    return centred * lax.rsqrt(spread + EPSILON)


def project(values, weight):
    return jnp.einsum("mnd,de->mne", values, weight, preferred_element_type=jnp.float32)


def fetch_rim(state, send_weight):
    outgoing = project(state, send_weight).astype(jnp.bfloat16)
    extended = with_halo(outgoing, (("dom", 1),), HB * BLK)
    return extended


def update_nodes(state, sender_terms, sender_rows, matrices, bias_pair, gain_pair):
    batch_size, node_count, width_d = state.shape
    slot_count = sender_rows.shape[1]
    receiver_terms = project(state, matrices[1]) + bias_pair[0]
    picked = jnp.take(sender_terms, sender_rows.reshape(-1), axis=1).reshape(
        batch_size, node_count, slot_count, width_d
    )
    pre_act = picked.astype(jnp.float32) + receiver_terms[:, :, None, :]
    hidden = jax.nn.silu(pre_act).astype(jnp.bfloat16)
    edge_out = jnp.einsum("mnkd,de->mnke", hidden, matrices[2], preferred_element_type=jnp.float32)
    messages = jnp.sum(layer_norm(edge_out) * gain_pair[0], axis=2).astype(jnp.bfloat16)
    node_pre = project(state, matrices[3]) + project(messages, matrices[4]) + bias_pair[1]
    node_hidden = jax.nn.silu(node_pre).astype(jnp.bfloat16)
    node_out = project(node_hidden, matrices[5])
    return (state.astype(jnp.float32) + layer_norm(node_out) * gain_pair[1]).astype(jnp.bfloat16)


def in_rounds(members, layer_mats, biases, norm_gains, edge_blocks, edge_shift):
    blocks = edge_blocks.shape[0]
    block_rows = jnp.repeat(edge_blocks, BLK, axis=0)
    row_offsets = jnp.repeat(edge_shift, BLK, axis=0)
    positions = (jnp.arange(blocks * BLK, dtype=jnp.int32) % BLK)[:, None]
    sender_rows = block_rows * BLK + (positions + row_offsets) % BLK
    sections = lax.axis_size("section")
    section_index = lax.axis_index("section")
    matrices = layer_mats[0]
    bias_pair = biases[0]
    gain_pair = norm_gains[0]

    def advance(moment, state):
        anchor = (section_index - moment) % sections
        entry_tick = (sections - anchor) % sections
        active = jnp.logical_and(moment >= entry_tick, moment - entry_tick < sections)
        sender_terms = fetch_rim(state, matrices[0])
        state = lax.cond(
            active,
            lambda: update_nodes(state, sender_terms, sender_rows, matrices, bias_pair, gain_pair),
            lambda: state,
        )
        return from_behind(state, "section", 1)

    final_state = lax.fori_loop(0, 2 * sections, advance, members)
    member_count = final_state.shape[0] * sections * lax.axis_size("ens")
    member_total = lax.psum(
        jnp.sum(final_state.astype(jnp.float32), axis=0).astype(jnp.bfloat16), ("section", "ens")
    ).astype(jnp.float32)
    return (final_state, member_total / member_count)


def silu(v):
    half = 0.5 * v
    return half + half * jnp.tanh(half)


def norm(v):
    scale = 1.0 / v.shape[-1]
    centred = v - jnp.sum(v, axis=-1, keepdims=True) * scale
    spread = jnp.sum(centred * centred, axis=-1, keepdims=True) * scale
    return centred * lax.rsqrt(spread + EPSILON)


def dot(a, b):
    return jnp.dot(a, b, preferred_element_type=F32)


def shifted_block(senders, block, shift):
    width = senders.shape[2]
    base = pl.multiple_of((shift // 8) * 8, 8)
    rest = shift % 8
    rows = senders[block, pl.ds(base, BLK + 8), :].reshape(BLK // 8 + 1, 8, width)
    turned = pltpu.roll(rows, (8 - rest) % 8, 1)
    place = lax.broadcasted_iota(jnp.int32, (1, 8, width), 1)
    return jnp.where(place < 8 - rest, turned[:-1], turned[1:]).reshape(BLK, width)


PIECE = 384
RIDERS = 16
SIDES = 8


def prepare_kernel(start, members, lists, mats, terms, parcel, piece, sem):
    at = pl.multiple_of(start[0], BLK)
    copy = pltpu.make_async_copy(mats.at[pl.ds(at, PIECE), :], piece.at[pl.ds(0, PIECE), :], sem)
    copy.start()
    width = members.shape[1]
    parcel[0:BLK] = members[...]
    parcel[BLK:] = jnp.broadcast_to(lists[...], (16, width)).astype(BF16)
    rest = terms[...]
    rows = []
    for _ in range(3):
        head = rest.astype(BF16)
        rows.append(head.astype(F32))
        rest = rest - rows[-1]
    rows.append(jnp.zeros_like(rest))
    piece[PIECE:] = jnp.concatenate(rows, axis=0).astype(BF16)
    copy.wait()


def prepare(start, members, lists, mats, terms):
    width = members.shape[1]
    smem = pl.BlockSpec(memory_space=pltpu.SMEM)
    vmem = pl.BlockSpec(memory_space=pltpu.VMEM)
    return pl.pallas_call(
        prepare_kernel,
        out_shape=[
            jax.ShapeDtypeStruct((BLK + 16, width), BF16),
            jax.ShapeDtypeStruct((PIECE + RIDERS, width), BF16),
        ],
        in_specs=[smem, vmem, vmem, pl.BlockSpec(memory_space=pl.ANY), vmem],
        out_specs=[vmem, vmem],
        scratch_shapes=[pltpu.SemaphoreType.DMA(())],
    )(start, members, lists, mats, terms)


def layer_kernel(targets, slots, states, sources, *refs):
    where, table = refs[:2]
    refs = refs[2:]
    state_refs, refs = refs[:states], refs[states:]
    own, own_terms = refs[:2]
    refs = refs[2:]
    gathered, refs = refs[: SIDES * sources], refs[SIDES * sources :]
    out, mats, riders, senders, hidden, sems = refs
    width = out.shape[1]
    blocks = senders.shape[0]

    def load(i, x, at, rows, to):
        return pltpu.make_async_copy(x.at[pl.ds(at, rows), :], mats.at[pl.ds(to, rows), :], sems.at[i])

    for source in range(sources + 1):

        @pl.when(where[0] == source)
        def _():
            for i in range(SIDES):
                if source == 0:
                    load(i, own, i * PIECE, PIECE, i * PIECE).start()
                else:
                    to = pl.multiple_of(where[1 + i], BLK)
                    load(i, gathered[(source - 1) * SIDES + i], 0, PIECE, to).start()
            back = own_terms if source == 0 else gathered[(source - 1) * SIDES]
            pltpu.make_async_copy(back.at[pl.ds(PIECE, RIDERS), :], riders, sems.at[SIDES]).start()

    if states == 1:
        state = state_refs[0][0 : blocks * BLK]
    else:
        state = jnp.concatenate([x[0:BLK] for x in state_refs], axis=0)
    for i in range(SIDES):
        load(i, own, i * PIECE, PIECE, i * PIECE).wait()
    pltpu.make_async_copy(own_terms.at[pl.ds(PIECE, RIDERS), :], riders, sems.at[SIDES]).wait()
    rows = riders[...].astype(F32)
    terms = rows[0:4] + rows[4:8] + rows[8:12]

    def mat(i):
        return mats[i * width : (i + 1) * width, :]

    sent = dot(state, mat(0)).astype(BF16).astype(F32)
    for b in range(blocks):
        block = sent[b * BLK : (b + 1) * BLK]
        senders[b, 0:BLK] = block
        senders[b, BLK : 2 * BLK] = block
    nodes = targets * BLK
    state = state[0:nodes]
    received = dot(state, mat(1)) + terms[0:1]
    collected = []
    for b in range(targets):
        for k in range(slots):
            block = table[b * 2 * slots + k]
            shift = table[b * 2 * slots + slots + k]
            v = shifted_block(senders, block, shift) + received[b * BLK : (b + 1) * BLK]
            hidden[b, k * BLK : (k + 1) * BLK] = silu(v).astype(BF16)
        e = dot(hidden[b], mat(2))
        total = norm(e[0:BLK])
        for k in range(1, slots):
            total += norm(e[k * BLK : (k + 1) * BLK])
        collected.append((total * terms[2:3]).astype(BF16))
    messages = jnp.concatenate(collected, axis=0)
    pre = dot(state, mat(3)) + dot(messages, mat(4)) + terms[1:2]
    node_out = dot(silu(pre).astype(BF16), mat(5))
    out[...] = (state.astype(F32) + norm(node_out) * terms[3:4]).astype(BF16)


def run_layer(states, blocks, targets, table, slots, where, own, own_terms, gathered):
    width = own.shape[1]
    sources = len(gathered) // SIDES
    smem = pl.BlockSpec(memory_space=pltpu.SMEM)
    vmem = pl.BlockSpec(memory_space=pltpu.VMEM)
    anyw = pl.BlockSpec(memory_space=pl.ANY)
    return pl.pallas_call(
        functools.partial(layer_kernel, targets, slots, len(states), sources),
        out_shape=jax.ShapeDtypeStruct((targets * BLK, width), BF16),
        in_specs=[smem, smem] + [vmem] * len(states) + [anyw] * (2 + len(gathered)),
        out_specs=vmem,
        scratch_shapes=[
            pltpu.VMEM((MATS * width, width), BF16),
            pltpu.VMEM((RIDERS, width), BF16),
            pltpu.VMEM((blocks, 2 * BLK + 8, width), F32),
            pltpu.VMEM((targets, slots * BLK, width), BF16),
            pltpu.SemaphoreType.DMA((SIDES + 1,)),
        ],
        cost_estimate=pl.CostEstimate(
            flops=2 * targets * BLK * (slots + 5) * width * width,
            bytes_accessed=2 * MATS * width * width,
            transcendentals=targets * BLK * slots * width,
        ),
        compiler_params=pltpu.CompilerParams(vmem_limit_bytes=32 << 20),
    )(where, table, *states, own, own_terms, *gathered)


def at_home(members, layer_mats, biases, norm_gains, edge_blocks, edge_shift):
    doms, cores = lax.axis_size("dom"), lax.axis_size("ens")
    layers = lax.axis_size("section")
    s, d, e = (lax.axis_index(a) for a in AXES)
    slots = edge_blocks.shape[1]
    width = members.shape[2]
    mats = layer_mats[0].reshape(MATS * width, width)
    spots = [(i, j, k) for i in range(layers) for j in range(doms) for k in range(cores)]

    def index(i, j, k):
        return (i * doms + j) * cores + k

    def swap(x, by):
        a, b, c = by
        return lax.ppermute(x, AXES, [(index(i, j, k), index(i ^ a, j ^ b, k ^ c)) for i, j, k in spots])

    lists = jnp.concatenate([edge_blocks, edge_shift], axis=1)
    lists = jnp.pad(lists, ((0, 0), (0, width - 2 * slots))).astype(F32)
    terms = jnp.concatenate([biases[0], norm_gains[0]], axis=0)
    start = jnp.reshape((d * cores + e) * PIECE, (1,)).astype(jnp.int32)
    parcel, piece = prepare(start, members[0], lists, mats, terms)

    order = (0, 1, 3, 2)
    low = s < 2
    third = swap(piece, (3, 0, 0))
    states = [parcel] + [swap(parcel, (0, r, 0)) for r in order[1:]]
    first = swap(jnp.where(low, piece, third), (1, 0, 0))
    second = swap(jnp.where(low, third, piece), (1, 0, 0))

    rows = jnp.concatenate([x[BLK : BLK + 1, : 2 * slots] for x in states], axis=0).astype(jnp.int32)
    block_of = d ^ jnp.array(order, jnp.int32)[:, None]
    away = ((block_of + rows[:, :slots] + (doms - HB)) % doms) ^ d
    place = jnp.where(away == 3, 2, jnp.where(away == 2, 3, away))
    table = jnp.concatenate([place, rows[:, slots:]], axis=1).reshape(-1)

    def spread(x, along):
        near, far = swap(x, (0, 1, 0)), swap(x, (0, 2, 0))
        both = swap(far, (0, 1, 0)) if along == 1 else swap(near, (0, 2, 0))
        mine = [x, near, far, both]
        return mine + [swap(p, (0, 0, 1)) for p in mine]

    third, first, second = spread(third, 1), spread(first, 2), spread(second, 1)
    places = jnp.stack([((d ^ r) * cores + (e ^ q)) * PIECE for q in (0, 1) for r in range(doms)])

    def where(*source):
        pick = jnp.array(source, jnp.int32)[s]
        return jnp.concatenate([pick[None], places.astype(jnp.int32)])

    run = functools.partial(run_layer, table=table, slots=slots, own=mats, own_terms=piece)
    state = run(states, 4, 4, where=where(0, 2, 2, 1), gathered=third + first)
    state = run([state], 4, 4, where=where(2, 0, 1, 2), gathered=third + first)
    state = run([state], 4, 3, where=where(2, 1, 0, 2), gathered=third + second)
    state = run([state], 3, 1, where=where(1, 2, 2, 0), gathered=third + second)

    total = state
    for by in ((0, 0, 1), (1, 0, 0)):
        total = (total.astype(F32) + swap(total, by).astype(F32)).astype(BF16)
    total = total.astype(F32) + swap(total, (2, 0, 0)).astype(F32)
    count = members.shape[0] * layers * cores
    return (state[None], total / count)


def solution(mesh):
    shape = dict(mesh.shape)
    placed = (
        P(("section", "ens"), "dom", None),
        P("section", None, None, None),
        P("section", None, None),
        P("section", None, None),
        P("dom", None),
        P("dom", None),
    )

    def on_device(members, layer_mats, biases, norm_gains, edge_blocks, edge_shift):
        small = shape["section"] == 4 and shape["dom"] == 4 and shape["ens"] == 2
        one_each = members.shape[:2] == (1, BLK) and layer_mats.shape[0] == 1
        one_each = one_each and MATS * members.shape[2] == SIDES * PIECE
        plan = at_home if small and one_each else in_rounds
        return plan(members, layer_mats, biases, norm_gains, edge_blocks, edge_shift)

    return jax.shard_map(
        on_device,
        mesh=mesh,
        in_specs=placed,
        out_specs=(P(("section", "ens"), "dom", None), P("dom", None)),
        check_vma=False,
    )
```

```python
import functools

import jax
import jax.numpy as jnp
from jax import lax
from jax.experimental import pallas as pl
from jax.experimental.pallas import tpu as pltpu
from jax.sharding import PartitionSpec as P

BLK = 128
HB = 1
EPSILON = 1e-05
MATS = 6
F32 = jnp.float32
BF16 = jnp.bfloat16
AXES = ("section", "dom", "ens")


def with_halo(x, sides, width):
    for axis, dim in sides:
        devices, length = (lax.axis_size(axis), x.shape[dim])
        up = [(i, (i + 1) % devices) for i in range(devices)]
        down = [(j, i) for i, j in up]
        last = lax.slice_in_dim(x, length - width, length, axis=dim)
        first = lax.slice_in_dim(x, 0, width, axis=dim)
        before = lax.ppermute(last, axis, up)
        after = lax.ppermute(first, axis, down)
        x = jnp.concatenate([before, x, after], axis=dim)
    return x


def from_behind(x, axis, by):
    devices = lax.axis_size(axis)
    return lax.ppermute(x, axis, [(i, (i + by) % devices) for i in range(devices)])


def layer_norm(values):
    average = jnp.mean(values, axis=-1, keepdims=True)
    centred = values - average
    spread = jnp.mean(centred * centred, axis=-1, keepdims=True)
    return centred * lax.rsqrt(spread + EPSILON)


def project(values, weight):
    return jnp.einsum("mnd,de->mne", values, weight, preferred_element_type=jnp.float32)


def fetch_rim(state, send_weight):
    outgoing = project(state, send_weight).astype(jnp.bfloat16)
    extended = with_halo(outgoing, (("dom", 1),), HB * BLK)
    return extended


def update_nodes(state, sender_terms, sender_rows, matrices, bias_pair, gain_pair):
    batch_size, node_count, width_d = state.shape
    slot_count = sender_rows.shape[1]
    receiver_terms = project(state, matrices[1]) + bias_pair[0]
    picked = jnp.take(sender_terms, sender_rows.reshape(-1), axis=1).reshape(
        batch_size, node_count, slot_count, width_d
    )
    pre_act = picked.astype(jnp.float32) + receiver_terms[:, :, None, :]
    hidden = jax.nn.silu(pre_act).astype(jnp.bfloat16)
    edge_out = jnp.einsum("mnkd,de->mnke", hidden, matrices[2], preferred_element_type=jnp.float32)
    messages = jnp.sum(layer_norm(edge_out) * gain_pair[0], axis=2).astype(jnp.bfloat16)
    node_pre = project(state, matrices[3]) + project(messages, matrices[4]) + bias_pair[1]
    node_hidden = jax.nn.silu(node_pre).astype(jnp.bfloat16)
    node_out = project(node_hidden, matrices[5])
    return (state.astype(jnp.float32) + layer_norm(node_out) * gain_pair[1]).astype(jnp.bfloat16)


def in_rounds(members, layer_mats, biases, norm_gains, edge_blocks, edge_shift):
    blocks = edge_blocks.shape[0]
    block_rows = jnp.repeat(edge_blocks, BLK, axis=0)
    row_offsets = jnp.repeat(edge_shift, BLK, axis=0)
    positions = (jnp.arange(blocks * BLK, dtype=jnp.int32) % BLK)[:, None]
    sender_rows = block_rows * BLK + (positions + row_offsets) % BLK
    sections = lax.axis_size("section")
    section_index = lax.axis_index("section")
    matrices = layer_mats[0]
    bias_pair = biases[0]
    gain_pair = norm_gains[0]

    def advance(moment, state):
        anchor = (section_index - moment) % sections
        entry_tick = (sections - anchor) % sections
        active = jnp.logical_and(moment >= entry_tick, moment - entry_tick < sections)
        sender_terms = fetch_rim(state, matrices[0])
        state = lax.cond(
            active,
            lambda: update_nodes(state, sender_terms, sender_rows, matrices, bias_pair, gain_pair),
            lambda: state,
        )
        return from_behind(state, "section", 1)

    final_state = lax.fori_loop(0, 2 * sections, advance, members)
    member_count = final_state.shape[0] * sections * lax.axis_size("ens")
    member_total = lax.psum(
        jnp.sum(final_state.astype(jnp.float32), axis=0).astype(jnp.bfloat16), ("section", "ens")
    ).astype(jnp.float32)
    return (final_state, member_total / member_count)


def silu(v):
    half = 0.5 * v
    return half + half * jnp.tanh(half)


def norm(v):
    scale = 1.0 / v.shape[-1]
    centred = v - jnp.sum(v, axis=-1, keepdims=True) * scale
    spread = jnp.sum(centred * centred, axis=-1, keepdims=True) * scale
    return centred * lax.rsqrt(spread + EPSILON)


def dot(a, b):
    return jnp.dot(a, b, preferred_element_type=F32)


def shifted_block(senders, block, shift):
    width = senders.shape[2]
    base = pl.multiple_of((shift // 8) * 8, 8)
    rest = shift % 8
    rows = senders[block, pl.ds(base, BLK + 8), :].reshape(BLK // 8 + 1, 8, width)
    turned = pltpu.roll(rows, (8 - rest) % 8, 1)
    place = lax.broadcasted_iota(jnp.int32, (1, 8, width), 1)
    return jnp.where(place < 8 - rest, turned[:-1], turned[1:]).reshape(BLK, width)


RIDERS = 16
ENTRY = 0
SECOND = 2


def call(kernel, out_shape, args, spaces, scratch=(), flops=0, **kwargs):
    specs = [pl.BlockSpec(memory_space=x) for x in spaces]
    outs = jax.tree.map(lambda _: pl.BlockSpec(memory_space=pltpu.VMEM), out_shape)
    return pl.pallas_call(
        functools.partial(kernel, **kwargs),
        out_shape=out_shape,
        in_specs=specs,
        out_specs=outs,
        scratch_shapes=list(scratch),
        cost_estimate=pl.CostEstimate(flops=flops, bytes_accessed=1 << 20, transcendentals=0),
        compiler_params=pltpu.CompilerParams(vmem_limit_bytes=32 << 20),
    )(*args)


def parcel_kernel(members, blocks, shifts, parcel, lists):
    slots = blocks.shape[1]
    lists[...] = jnp.zeros_like(lists)
    lists[0:1, 0:slots] = blocks[...].astype(F32)
    lists[8:9, 0:slots] = shifts[...].astype(F32)
    parcel[0:BLK] = members[...]
    parcel[BLK:] = lists[...].astype(BF16)


def addends(values):
    rows, rest = [], values
    for _ in range(3):
        head = rest.astype(BF16).astype(F32)
        rows.append(head)
        rest = rest - head
    rows.append(jnp.zeros_like(rest))
    return jnp.concatenate(rows, axis=0).astype(BF16)


def halves_kernel(core, mats, biases, gains, early, late, sems):
    part = late.shape[0]
    at = pl.multiple_of(core[0] * part, BLK)
    copies = [
        pltpu.make_async_copy(mats.at[pl.ds(at, part), :], early.at[pl.ds(0, part), :], sems.at[0]),
        pltpu.make_async_copy(mats.at[pl.ds(at + 2 * part, part), :], late, sems.at[1]),
    ]
    for copy in copies:
        copy.start()
    early[part:] = addends(jnp.concatenate([biases[...], gains[...]], axis=0))
    for copy in copies:
        copy.wait()


def layers_kernel(*refs, slots, fresh, own, given, split):
    place = refs[0]
    refs = refs[1:]
    count = 4 if fresh else 1
    inputs, refs = refs[:count], refs[count:]
    if own:
        mats, biases, gains = refs[:3]
        refs = refs[3:]
    if given:
        parts, refs = refs[:4], refs[4:]
    outs, refs = (refs[:4], refs[4:]) if split else (refs[:1], refs[1:])
    loaded, riders, senders, hidden, words, table, sems = refs
    width = senders.shape[2]
    nodes = 4 * BLK
    d, e = place[0], place[1]
    part = MATS * width // 4
    plans = []
    if own:
        plans.append(
            [
                pltpu.make_async_copy(mats.at[pl.ds(i * part, part), :], loaded.at[0, pl.ds(i * part, part), :], sems.at[i])
                for i in range(4)
            ]
        )
    if given:
        slot = len(plans)
        copies = []
        for i, x in enumerate(parts):
            row = pl.multiple_of((i // 2 * 2 + (e if i % 2 == 0 else 1 - e)) * part, BLK)
            copies.append(
                pltpu.make_async_copy(
                    x.at[pl.ds(0, part), :], loaded.at[slot, pl.ds(row, part), :], sems.at[4 * slot + i]
                )
            )
        copies.append(pltpu.make_async_copy(parts[0].at[pl.ds(part, RIDERS), :], riders, sems.at[8]))
        plans.append(copies)
    for copies in plans:
        for copy in copies:
            copy.start()

    if fresh:
        state = jnp.concatenate([x[0:BLK] for x in inputs], axis=0)
        rows = []
        for r in range(4):
            lists = inputs[r][BLK:].astype(F32).astype(jnp.int32)[:, 0:128]
            sender = ((d ^ r) + lists[0:1] + (4 - HB)) % 4 ^ d
            rows += [sender, lists[8:9]]
        numbers = jnp.concatenate(rows, axis=0)
    else:
        state = inputs[0][0:nodes]
        numbers = inputs[0][nodes:].astype(F32).astype(jnp.int32)[0:8, 0:128]
    words[...] = numbers
    to_scalars = pltpu.make_async_copy(words, table, sems.at[9])
    to_scalars.start()

    for at, copies in enumerate(plans):
        last_layer = at == len(plans) - 1
        if own and at == 0:
            terms = jnp.concatenate([biases[...], gains[...]], axis=0)
            for copy in copies[:2]:
                copy.wait()
            later = copies[2:]
        else:
            copies[0].wait()
            copies[1].wait()
            copies[4].wait()
            values = riders[...].astype(F32)
            terms = values[0:4] + values[4:8] + values[8:12]
            later = copies[2:4]

        def mat(i):
            return loaded[at, i * width : (i + 1) * width, :]

        sent = dot(state, mat(0)).astype(BF16).astype(F32)
        for b in range(4):
            block = sent[b * BLK : (b + 1) * BLK]
            senders[b, 0:BLK] = block
            senders[b, BLK : 2 * BLK] = block
        received = dot(state, mat(1)) + terms[0:1]
        if at == 0:
            to_scalars.wait()
        collected = []
        for b in range(4):
            for k in range(slots):
                v = shifted_block(senders, table[2 * b, k], table[2 * b + 1, k]) + received[b * BLK : (b + 1) * BLK]
                hidden[b, k * BLK : (k + 1) * BLK] = silu(v).astype(BF16)
            edge = dot(hidden[b], mat(2))
            total = norm(edge[0:BLK])
            for k in range(1, slots):
                total += norm(edge[k * BLK : (k + 1) * BLK])
            collected.append((total * terms[2:3]).astype(BF16))
        messages = jnp.concatenate(collected, axis=0)
        for copy in later:
            copy.wait()
        pre = dot(state, mat(3)) + dot(messages, mat(4)) + terms[1:2]
        node_out = dot(silu(pre).astype(BF16), mat(5))
        state = (state.astype(F32) + norm(node_out) * terms[3:4]).astype(BF16)
        if last_layer and split:
            for b in range(4):
                outs[b][...] = state[b * BLK : (b + 1) * BLK]
        elif last_layer:
            outs[0][0:nodes] = state
            spare = jnp.zeros((16 - 8, 128), F32)
            outs[0][nodes:, 0:128] = jnp.concatenate([numbers.astype(F32), spare], axis=0).astype(BF16)
            outs[0][nodes:, 128:] = jnp.zeros((16, width - 128), BF16)


def run_layers(place, inputs, slots, own=None, given=None, split=False):
    width = inputs[0].shape[1]
    smem, vmem, anyw = pltpu.SMEM, pltpu.VMEM, pl.ANY
    args, spaces = [place] + inputs, [smem] + [vmem] * len(inputs)
    if own:
        args, spaces = args + list(own), spaces + [anyw, vmem, vmem]
    if given:
        args, spaces = args + list(given), spaces + [anyw] * 4
    layers = (own is not None) + (given is not None)
    block = jax.ShapeDtypeStruct((BLK, width), BF16)
    whole = jax.ShapeDtypeStruct((4 * BLK + 16, width), BF16)
    return call(
        layers_kernel,
        [block] * 4 if split else whole,
        args,
        spaces,
        scratch=[
            pltpu.VMEM((layers, MATS * width, width), BF16),
            pltpu.VMEM((RIDERS, width), BF16),
            pltpu.VMEM((4, 2 * BLK + 8, width), F32),
            pltpu.VMEM((4, slots * BLK, width), BF16),
            pltpu.VMEM((8, 128), jnp.int32),
            pltpu.SMEM((8, 128), jnp.int32),
            pltpu.SemaphoreType.DMA((10,)),
        ],
        flops=layers * 2 * 4 * BLK * (slots + 5) * width * width,
        slots=slots,
        fresh=len(inputs) == 4,
        own=own is not None,
        given=given is not None,
        split=split,
    )


def messages_kernel(place, *refs, targets):
    blocks, refs = refs[:4], refs[4:]
    outs, held = refs[:-1], refs[-1]
    total = jnp.zeros(blocks[0].shape, F32)
    for r, block in enumerate(blocks):
        held[r] = block[...]
        total += block[...].astype(F32)
    for out, section in zip(outs, targets):
        out[0:BLK] = held[place[0] ^ section]
        out[BLK:] = total.astype(BF16)


def in_two_stages(members, layer_mats, biases, norm_gains, edge_blocks, edge_shift):
    doms, cores = lax.axis_size("dom"), lax.axis_size("ens")
    layers = lax.axis_size("section")
    s, d, e = (lax.axis_index(a) for a in AXES)
    slots = edge_blocks.shape[1]
    width = members.shape[2]
    mats = layer_mats[0].reshape(MATS * width, width)
    part = MATS * width // 4
    place = jnp.stack([d, e]).astype(jnp.int32)
    smem, vmem, anyw = pltpu.SMEM, pltpu.VMEM, pl.ANY
    spots = [(i, j, k) for i in range(layers) for j in range(doms) for k in range(cores)]

    def shape(rows):
        return jax.ShapeDtypeStruct((rows, width), BF16)

    def index(i, j, k):
        return (i * doms + j) * cores + k

    def send(x, pairs):
        return lax.ppermute(x, AXES, [(index(*a), index(*b)) for a, b in pairs])

    def swap(x, by):
        a, b, c = by
        return send(x, [((i, j, k), (i ^ a, j ^ b, k ^ c)) for i, j, k in spots])

    def hop(x, source, target):
        return send(x, [((source, j, k), (target, j, k)) for i, j, k in spots if i == source])

    parcel = call(
        parcel_kernel,
        shape(BLK + 16),
        (members[0], edge_blocks, edge_shift),
        [vmem] * 3,
        [pltpu.VMEM((16, width), F32)],
    )
    arrived = [
        send(parcel, [((i, i ^ r, k), (ENTRY, i, k)) for i in range(layers) for k in range(cores)])
        for r in range(doms)
    ]

    early, late = call(
        halves_kernel,
        [shape(part + RIDERS), shape(part)],
        (place[1:], mats, biases[0], norm_gains[0]),
        [smem, anyw, vmem, vmem],
        [pltpu.SemaphoreType.DMA((2,))],
    )
    early, late = swap(early, (1, 0, 0)), swap(late, (1, 0, 0))

    own = (mats, biases[0], norm_gains[0])
    state = run_layers(place, arrived, slots, own=own)
    early, state = lax.optimization_barrier((early, state))
    early_mate = swap(early, (0, 0, 1))
    late_mate = swap(late, (0, 0, 1))
    given = (early, early_mate, late, late_mate)
    state = run_layers(place, [state], slots, given=given)
    state = hop(state, ENTRY, SECOND)
    blocks = run_layers(place, [state], slots, own=own, given=given, split=True)

    columns = [blocks[0]] + [swap(blocks[r], (0, r, 0)) for r in range(1, doms)]
    targets = [i for i in range(layers) if i != SECOND] + [SECOND]
    packed = call(
        messages_kernel,
        [shape(2 * BLK)] * layers,
        (place, *columns),
        [smem] + [vmem] * doms,
        [pltpu.VMEM((doms, BLK, width), BF16)],
        targets=targets,
    )
    final = packed[-1]
    for i, message in zip(targets[:-1], packed):
        final = jnp.where(s == i, hop(message, SECOND, i), final)
    total = final[BLK:]
    total = total.astype(F32) + swap(total, (0, 0, 1)).astype(F32)
    count = members.shape[0] * layers * cores
    return (final[None, :BLK], total / count)


def solution(mesh):
    shape = dict(mesh.shape)
    placed = (
        P(("section", "ens"), "dom", None),
        P("section", None, None, None),
        P("section", None, None),
        P("section", None, None),
        P("dom", None),
        P("dom", None),
    )

    def on_device(members, layer_mats, biases, norm_gains, edge_blocks, edge_shift):
        small = shape["section"] == 4 and shape["dom"] == 4 and shape["ens"] == 2
        one_each = members.shape[:2] == (1, BLK) and layer_mats.shape[0] == 1
        plan = in_two_stages if small and one_each else in_rounds
        return plan(members, layer_mats, biases, norm_gains, edge_blocks, edge_shift)

    return jax.shard_map(
        on_device,
        mesh=mesh,
        in_specs=placed,
        out_specs=(P(("section", "ens"), "dom", None), P("dom", None)),
        check_vma=False,
    )
```

```python
import functools

import jax
import jax.numpy as jnp
from jax import lax
from jax.experimental import pallas as pl
from jax.experimental.pallas import tpu as pltpu
from jax.sharding import PartitionSpec as P

BLK = 128
HB = 1
EPSILON = 1e-05
MATS = 6
F32 = jnp.float32
BF16 = jnp.bfloat16
AXES = ("section", "dom", "ens")


def with_halo(x, sides, width):
    for axis, dim in sides:
        devices, length = (lax.axis_size(axis), x.shape[dim])
        up = [(i, (i + 1) % devices) for i in range(devices)]
        down = [(j, i) for i, j in up]
        last = lax.slice_in_dim(x, length - width, length, axis=dim)
        first = lax.slice_in_dim(x, 0, width, axis=dim)
        before = lax.ppermute(last, axis, up)
        after = lax.ppermute(first, axis, down)
        x = jnp.concatenate([before, x, after], axis=dim)
    return x


def from_behind(x, axis, by):
    devices = lax.axis_size(axis)
    return lax.ppermute(x, axis, [(i, (i + by) % devices) for i in range(devices)])


def layer_norm(values):
    average = jnp.mean(values, axis=-1, keepdims=True)
    centred = values - average
    spread = jnp.mean(centred * centred, axis=-1, keepdims=True)
    return centred * lax.rsqrt(spread + EPSILON)


def project(values, weight):
    return jnp.einsum("mnd,de->mne", values, weight, preferred_element_type=jnp.float32)


def fetch_rim(state, send_weight):
    outgoing = project(state, send_weight).astype(jnp.bfloat16)
    extended = with_halo(outgoing, (("dom", 1),), HB * BLK)
    return extended


def update_nodes(state, sender_terms, sender_rows, matrices, bias_pair, gain_pair):
    batch_size, node_count, width_d = state.shape
    slot_count = sender_rows.shape[1]
    receiver_terms = project(state, matrices[1]) + bias_pair[0]
    picked = jnp.take(sender_terms, sender_rows.reshape(-1), axis=1).reshape(
        batch_size, node_count, slot_count, width_d
    )
    pre_act = picked.astype(jnp.float32) + receiver_terms[:, :, None, :]
    hidden = jax.nn.silu(pre_act).astype(jnp.bfloat16)
    edge_out = jnp.einsum("mnkd,de->mnke", hidden, matrices[2], preferred_element_type=jnp.float32)
    messages = jnp.sum(layer_norm(edge_out) * gain_pair[0], axis=2).astype(jnp.bfloat16)
    node_pre = project(state, matrices[3]) + project(messages, matrices[4]) + bias_pair[1]
    node_hidden = jax.nn.silu(node_pre).astype(jnp.bfloat16)
    node_out = project(node_hidden, matrices[5])
    return (state.astype(jnp.float32) + layer_norm(node_out) * gain_pair[1]).astype(jnp.bfloat16)


def in_rounds(members, layer_mats, biases, norm_gains, edge_blocks, edge_shift):
    blocks = edge_blocks.shape[0]
    block_rows = jnp.repeat(edge_blocks, BLK, axis=0)
    row_offsets = jnp.repeat(edge_shift, BLK, axis=0)
    positions = (jnp.arange(blocks * BLK, dtype=jnp.int32) % BLK)[:, None]
    sender_rows = block_rows * BLK + (positions + row_offsets) % BLK
    sections = lax.axis_size("section")
    section_index = lax.axis_index("section")
    matrices = layer_mats[0]
    bias_pair = biases[0]
    gain_pair = norm_gains[0]

    def advance(moment, state):
        anchor = (section_index - moment) % sections
        entry_tick = (sections - anchor) % sections
        active = jnp.logical_and(moment >= entry_tick, moment - entry_tick < sections)
        sender_terms = fetch_rim(state, matrices[0])
        state = lax.cond(
            active,
            lambda: update_nodes(state, sender_terms, sender_rows, matrices, bias_pair, gain_pair),
            lambda: state,
        )
        return from_behind(state, "section", 1)

    final_state = lax.fori_loop(0, 2 * sections, advance, members)
    member_count = final_state.shape[0] * sections * lax.axis_size("ens")
    member_total = lax.psum(
        jnp.sum(final_state.astype(jnp.float32), axis=0).astype(jnp.bfloat16), ("section", "ens")
    ).astype(jnp.float32)
    return (final_state, member_total / member_count)


def silu(v):
    half = 0.5 * v
    return half + half * jnp.tanh(half)


def norm(v):
    scale = 1.0 / v.shape[-1]
    centred = v - jnp.sum(v, axis=-1, keepdims=True) * scale
    spread = jnp.sum(centred * centred, axis=-1, keepdims=True) * scale
    return centred * lax.rsqrt(spread + EPSILON)


def dot(a, b):
    return jnp.dot(a, b, preferred_element_type=F32)


def shifted_block(senders, block, shift):
    width = senders.shape[2]
    base = pl.multiple_of((shift // 8) * 8, 8)
    rest = shift % 8
    rows = senders[block, pl.ds(base, BLK + 8), :].reshape(BLK // 8 + 1, 8, width)
    turned = pltpu.roll(rows, (8 - rest) % 8, 1)
    place = lax.broadcasted_iota(jnp.int32, (1, 8, width), 1)
    return jnp.where(place < 8 - rest, turned[:-1], turned[1:]).reshape(BLK, width)


RIDERS = 16
SECOND = 2


def call(kernel, out_shape, args, spaces, scratch=(), flops=0, **kwargs):
    specs = [pl.BlockSpec(memory_space=x) for x in spaces]
    args = [pltpu.with_memory_space_constraint(x, at) if at == pltpu.HBM else x for x, at in zip(args, spaces)]
    outs = jax.tree.map(lambda _: pl.BlockSpec(memory_space=pltpu.VMEM), out_shape)
    return pl.pallas_call(
        functools.partial(kernel, **kwargs),
        out_shape=out_shape,
        in_specs=specs,
        out_specs=outs,
        scratch_shapes=list(scratch),
        cost_estimate=pl.CostEstimate(flops=flops, bytes_accessed=1 << 20, transcendentals=0),
        compiler_params=pltpu.CompilerParams(vmem_limit_bytes=32 << 20),
    )(*args)


def parcel_kernel(members, blocks, shifts, parcel, lists, words, sems):
    slots = blocks.shape[1]
    copies = [
        pltpu.make_async_copy(blocks, words.at[pl.ds(0, 1), :], sems.at[0]),
        pltpu.make_async_copy(shifts, words.at[pl.ds(8, 1), :], sems.at[1]),
        pltpu.make_async_copy(members, parcel.at[pl.ds(0, BLK), :], sems.at[2]),
    ]
    for copy in copies:
        copy.start()
    lists[...] = jnp.zeros_like(lists)
    copies[0].wait()
    copies[1].wait()
    lists[0:1, 0:slots] = words[0:1].astype(F32)
    lists[8:9, 0:slots] = words[8:9].astype(F32)
    parcel[BLK:] = lists[...].astype(BF16)
    copies[2].wait()


def addends(values):
    rows, rest = [], values
    for _ in range(3):
        head = rest.astype(BF16).astype(F32)
        rows.append(head)
        rest = rest - head
    rows.append(jnp.zeros_like(rest))
    return jnp.concatenate(rows, axis=0).astype(BF16)


def half_kernel(core, mats, biases, gains, half, terms, sems):
    part = half.shape[0] - RIDERS
    at = pl.multiple_of(core[0] * part, BLK)
    copies = [
        pltpu.make_async_copy(biases, terms.at[pl.ds(0, 2), :], sems.at[0]),
        pltpu.make_async_copy(gains, terms.at[pl.ds(2, 2), :], sems.at[1]),
        pltpu.make_async_copy(mats.at[pl.ds(at, part), :], half.at[pl.ds(0, part), :], sems.at[2]),
    ]
    for copy in copies:
        copy.start()
    copies[0].wait()
    copies[1].wait()
    half[part:] = addends(terms[...])
    copies[2].wait()


def layers_kernel(*refs, slots, fresh, given, split):
    place = refs[0]
    refs = refs[1:]
    count = 4 if fresh else 1
    inputs, refs = refs[:count], refs[count:]
    mats, biases, gains = refs[:3]
    refs = refs[3:]
    if given:
        parts, refs = refs[:2], refs[2:]
    outs, refs = (refs[:4], refs[4:]) if split else (refs[:1], refs[1:])
    loaded, own_terms, riders, senders, hidden, words, table, sems = refs[:8]
    width = senders.shape[2]
    nodes = 4 * BLK
    d, e = place[0], place[1]
    part = MATS * width // 4
    half = 2 * part
    plans = [
        [
            pltpu.make_async_copy(mats.at[pl.ds(i * part, part), :], loaded.at[0, pl.ds(i * part, part), :], sems.at[i])
            for i in range(4)
        ]
        + [
            pltpu.make_async_copy(biases, own_terms.at[pl.ds(0, 2), :], sems.at[4]),
            pltpu.make_async_copy(gains, own_terms.at[pl.ds(2, 2), :], sems.at[5]),
        ]
    ]
    if given:
        plans.append(
            [
                pltpu.make_async_copy(
                    x.at[pl.ds(0, half), :],
                    loaded.at[1, pl.ds(pl.multiple_of(row * half, BLK), half), :],
                    sems.at[6 + i],
                )
                for i, (x, row) in enumerate(zip(parts, (e, 1 - e)))
            ]
            + [pltpu.make_async_copy(parts[0].at[pl.ds(half, RIDERS), :], riders, sems.at[8])]
        )
    for copies in plans:
        for copy in copies:
            copy.start()

    if fresh:
        copies = [pltpu.make_async_copy(x, refs[8].at[r], sems.at[10 + r]) for r, x in enumerate(inputs)]
        for copy in copies:
            copy.start()
        for copy in copies:
            copy.wait()
        inputs = [refs[8].at[r] for r in range(4)]
        state = jnp.concatenate([x[0:BLK] for x in inputs], axis=0)
        rows = []
        for r in range(4):
            lists = inputs[r][BLK : BLK + 16].astype(F32).astype(jnp.int32)[:, 0:128]
            sender = ((d ^ r) + lists[0:1] + (4 - HB)) % 4 ^ d
            rows += [sender, lists[8:9]]
        numbers = jnp.concatenate(rows, axis=0)
    else:
        state = inputs[0][0:nodes]
        numbers = inputs[0][nodes:].astype(F32).astype(jnp.int32)[0:8, 0:128]
    words[...] = numbers
    to_scalars = pltpu.make_async_copy(words, table, sems.at[9])
    to_scalars.start()

    for at, copies in enumerate(plans):
        last_layer = at == len(plans) - 1
        if at == 0:
            for i in (0, 1, 4, 5):
                copies[i].wait()
            terms = own_terms[...]
            later = copies[2:4]
        else:
            for copy in copies:
                copy.wait()
            values = riders[...].astype(F32)
            terms = values[0:4] + values[4:8] + values[8:12]
            later = []

        def mat(i):
            return loaded[at, i * width : (i + 1) * width, :]

        sent = dot(state, mat(0)).astype(BF16).astype(F32)
        for b in range(4):
            block = sent[b * BLK : (b + 1) * BLK]
            senders[b, 0:BLK] = block
            senders[b, BLK : 2 * BLK] = block
        received = dot(state, mat(1)) + terms[0:1]
        if at == 0:
            to_scalars.wait()
        collected = []
        for b in range(4):
            for k in range(slots):
                v = shifted_block(senders, table[2 * b, k], table[2 * b + 1, k]) + received[b * BLK : (b + 1) * BLK]
                hidden[b, k * BLK : (k + 1) * BLK] = silu(v).astype(BF16)
            edge = dot(hidden[b], mat(2))
            total = norm(edge[0:BLK])
            for k in range(1, slots):
                total += norm(edge[k * BLK : (k + 1) * BLK])
            collected.append((total * terms[2:3]).astype(BF16))
        messages = jnp.concatenate(collected, axis=0)
        for copy in later:
            copy.wait()
        pre = dot(state, mat(3)) + dot(messages, mat(4)) + terms[1:2]
        node_out = dot(silu(pre).astype(BF16), mat(5))
        state = (state.astype(F32) + norm(node_out) * terms[3:4]).astype(BF16)
        if last_layer and split:
            for b in range(4):
                outs[b][...] = state[b * BLK : (b + 1) * BLK]
        elif last_layer:
            outs[0][0:nodes] = state
            spare = jnp.zeros((16 - 8, 128), F32)
            outs[0][nodes:, 0:128] = jnp.concatenate([numbers.astype(F32), spare], axis=0).astype(BF16)
            outs[0][nodes:, 128:] = jnp.zeros((16, width - 128), BF16)


def run_layers(place, inputs, slots, own, given=None, split=False):
    width = inputs[0].shape[1]
    smem, vmem, hbm = pltpu.SMEM, pltpu.VMEM, pltpu.HBM
    fresh = len(inputs) == 4
    args, spaces = [place] + inputs + list(own), [smem] + [pl.ANY if fresh else vmem] * len(inputs) + [hbm] * 3
    if given:
        args, spaces = args + list(given), spaces + [pl.ANY] * 2
    layers = 1 if given is None else 2
    block = jax.ShapeDtypeStruct((BLK, width), BF16)
    whole = jax.ShapeDtypeStruct((4 * BLK + 16, width), BF16)
    return call(
        layers_kernel,
        [block] * 4 if split else whole,
        args,
        spaces,
        scratch=[
            pltpu.VMEM((layers, MATS * width, width), BF16),
            pltpu.VMEM((4, width), F32),
            pltpu.VMEM((RIDERS, width), BF16),
            pltpu.VMEM((4, 2 * BLK + 8, width), F32),
            pltpu.VMEM((4, slots * BLK, width), BF16),
            pltpu.VMEM((8, 128), jnp.int32),
            pltpu.SMEM((8, 128), jnp.int32),
            pltpu.SemaphoreType.DMA((14,)),
        ]
        + [pltpu.VMEM((4, BLK + 16, width), BF16)] * fresh,
        flops=layers * 2 * 4 * BLK * (slots + 5) * width * width,
        slots=slots,
        fresh=fresh,
        given=given is not None,
        split=split,
    )


def messages_kernel(place, *refs, targets):
    blocks, refs = refs[:4], refs[4:]
    outs, held = refs[:-1], refs[-1]
    total = jnp.zeros(blocks[0].shape, F32)
    for r, block in enumerate(blocks):
        held[r] = block[...]
        total += block[...].astype(F32)
    for out, section in zip(outs, targets):
        out[0:BLK] = held[place[0] ^ section]
        out[BLK:] = total.astype(BF16)


def in_two_stages(members, layer_mats, biases, norm_gains, edge_blocks, edge_shift):
    doms, cores = lax.axis_size("dom"), lax.axis_size("ens")
    layers = lax.axis_size("section")
    s, d, e = (lax.axis_index(a) for a in AXES)
    slots = edge_blocks.shape[1]
    width = members.shape[2]
    mats = layer_mats[0].reshape(MATS * width, width)
    part = MATS * width // 4
    place = jnp.stack([d, e]).astype(jnp.int32)
    smem, vmem = pltpu.SMEM, pltpu.VMEM
    spots = [(i, j, k) for i in range(layers) for j in range(doms) for k in range(cores)]

    def shape(rows):
        return jax.ShapeDtypeStruct((rows, width), BF16)

    def index(i, j, k):
        return (i * doms + j) * cores + k

    def send(x, pairs):
        return lax.ppermute(x, AXES, [(index(*a), index(*b)) for a, b in pairs])

    def swap(x, by):
        a, b, c = by
        return send(x, [((i, j, k), (i ^ a, j ^ b, k ^ c)) for i, j, k in spots])

    def hop(x, source, target):
        return send(x, [((source, j, k), (target, j, k)) for i, j, k in spots if i == source])

    hbm = pltpu.HBM
    parcel = call(
        parcel_kernel,
        shape(BLK + 16),
        (members[0], edge_blocks, edge_shift),
        [hbm] * 3,
        [pltpu.VMEM((16, width), F32), pltpu.VMEM((16, slots), jnp.int32), pltpu.SemaphoreType.DMA((3,))],
    )
    arrived = [
        send(parcel, [((i, i ^ r, k), (0, i, k)) for i in range(layers) for k in range(cores)])
        for r in range(doms)
    ]

    own = (mats, biases[0], norm_gains[0])
    half = call(
        half_kernel,
        shape(2 * part + RIDERS),
        (place[1:], *own),
        [smem] + [hbm] * 3,
        [pltpu.VMEM((4, width), F32), pltpu.SemaphoreType.DMA((3,))],
    )
    half = hop(half, layers - 1, SECOND)

    state = run_layers(place, arrived, slots, own)
    state = hop(state, 0, 1)
    state = run_layers(place, [state], slots, own)
    half = lax.optimization_barrier((half, state))[0]
    given = (half, swap(half, (0, 0, 1)))
    state = hop(state, 1, SECOND)
    blocks = run_layers(place, [state], slots, own, given, split=True)

    columns = [blocks[0]] + [swap(blocks[r], (0, r, 0)) for r in range(1, doms)]
    targets = [i for i in range(layers) if i != SECOND] + [SECOND]
    packed = call(
        messages_kernel,
        [shape(2 * BLK)] * layers,
        (place, *columns),
        [smem] + [vmem] * doms,
        [pltpu.VMEM((doms, BLK, width), BF16)],
        targets=targets,
    )
    final = packed[-1]
    for i, message in zip(targets[:-1], packed):
        final = jnp.where(s == i, hop(message, SECOND, i), final)
    total = final[BLK:]
    total = total.astype(F32) + swap(total, (0, 0, 1)).astype(F32)
    count = members.shape[0] * layers * cores
    return (final[None, :BLK], total / count)


def solution(mesh):
    shape = dict(mesh.shape)
    placed = (
        P(("section", "ens"), "dom", None),
        P("section", None, None, None),
        P("section", None, None),
        P("section", None, None),
        P("dom", None),
        P("dom", None),
    )

    def on_device(members, layer_mats, biases, norm_gains, edge_blocks, edge_shift):
        small = shape["section"] == 4 and shape["dom"] == 4 and shape["ens"] == 2
        one_each = members.shape[:2] == (1, BLK) and layer_mats.shape[0] == 1
        plan = in_two_stages if small and one_each else in_rounds
        return plan(members, layer_mats, biases, norm_gains, edge_blocks, edge_shift)

    return jax.shard_map(
        on_device,
        mesh=mesh,
        in_specs=placed,
        out_specs=(P(("section", "ens"), "dom", None), P("dom", None)),
        check_vma=False,
    )
```

```python
import functools

import jax
import jax.numpy as jnp
from jax import lax
from jax.experimental import pallas as pl
from jax.experimental.pallas import tpu as pltpu
from jax.sharding import PartitionSpec as P

BLK = 128
HB = 1
EPSILON = 1e-05
MATS = 6
F32 = jnp.float32
BF16 = jnp.bfloat16
AXES = ("section", "dom", "ens")


def with_halo(x, sides, width):
    for axis, dim in sides:
        devices, length = (lax.axis_size(axis), x.shape[dim])
        up = [(i, (i + 1) % devices) for i in range(devices)]
        down = [(j, i) for i, j in up]
        last = lax.slice_in_dim(x, length - width, length, axis=dim)
        first = lax.slice_in_dim(x, 0, width, axis=dim)
        before = lax.ppermute(last, axis, up)
        after = lax.ppermute(first, axis, down)
        x = jnp.concatenate([before, x, after], axis=dim)
    return x


def from_behind(x, axis, by):
    devices = lax.axis_size(axis)
    return lax.ppermute(x, axis, [(i, (i + by) % devices) for i in range(devices)])


def layer_norm(values):
    average = jnp.mean(values, axis=-1, keepdims=True)
    centred = values - average
    spread = jnp.mean(centred * centred, axis=-1, keepdims=True)
    return centred * lax.rsqrt(spread + EPSILON)


def project(values, weight):
    return jnp.einsum("mnd,de->mne", values, weight, preferred_element_type=jnp.float32)


def fetch_rim(state, send_weight):
    outgoing = project(state, send_weight).astype(jnp.bfloat16)
    extended = with_halo(outgoing, (("dom", 1),), HB * BLK)
    return extended


def update_nodes(state, sender_terms, sender_rows, matrices, bias_pair, gain_pair):
    batch_size, node_count, width_d = state.shape
    slot_count = sender_rows.shape[1]
    receiver_terms = project(state, matrices[1]) + bias_pair[0]
    picked = jnp.take(sender_terms, sender_rows.reshape(-1), axis=1).reshape(
        batch_size, node_count, slot_count, width_d
    )
    pre_act = picked.astype(jnp.float32) + receiver_terms[:, :, None, :]
    hidden = jax.nn.silu(pre_act).astype(jnp.bfloat16)
    edge_out = jnp.einsum("mnkd,de->mnke", hidden, matrices[2], preferred_element_type=jnp.float32)
    messages = jnp.sum(layer_norm(edge_out) * gain_pair[0], axis=2).astype(jnp.bfloat16)
    node_pre = project(state, matrices[3]) + project(messages, matrices[4]) + bias_pair[1]
    node_hidden = jax.nn.silu(node_pre).astype(jnp.bfloat16)
    node_out = project(node_hidden, matrices[5])
    return (state.astype(jnp.float32) + layer_norm(node_out) * gain_pair[1]).astype(jnp.bfloat16)


def in_rounds(members, layer_mats, biases, norm_gains, edge_blocks, edge_shift):
    blocks = edge_blocks.shape[0]
    block_rows = jnp.repeat(edge_blocks, BLK, axis=0)
    row_offsets = jnp.repeat(edge_shift, BLK, axis=0)
    positions = (jnp.arange(blocks * BLK, dtype=jnp.int32) % BLK)[:, None]
    sender_rows = block_rows * BLK + (positions + row_offsets) % BLK
    sections = lax.axis_size("section")
    section_index = lax.axis_index("section")
    matrices = layer_mats[0]
    bias_pair = biases[0]
    gain_pair = norm_gains[0]

    def advance(moment, state):
        anchor = (section_index - moment) % sections
        entry_tick = (sections - anchor) % sections
        active = jnp.logical_and(moment >= entry_tick, moment - entry_tick < sections)
        sender_terms = fetch_rim(state, matrices[0])
        state = lax.cond(
            active,
            lambda: update_nodes(state, sender_terms, sender_rows, matrices, bias_pair, gain_pair),
            lambda: state,
        )
        return from_behind(state, "section", 1)

    final_state = lax.fori_loop(0, 2 * sections, advance, members)
    member_count = final_state.shape[0] * sections * lax.axis_size("ens")
    member_total = lax.psum(
        jnp.sum(final_state.astype(jnp.float32), axis=0).astype(jnp.bfloat16), ("section", "ens")
    ).astype(jnp.float32)
    return (final_state, member_total / member_count)


def silu(v):
    half = jnp.asarray(0.5, v.dtype) * v
    return half + half * jnp.tanh(half)


def norm(v):
    scale = 1.0 / v.shape[-1]
    centred = v - jnp.sum(v, axis=-1, keepdims=True) * scale
    spread = jnp.sum(centred * centred, axis=-1, keepdims=True) * scale
    return centred * lax.rsqrt(spread + EPSILON)


def dot(a, b):
    return jnp.dot(a, b, preferred_element_type=F32)


def shifted_block(senders, block, shift):
    width = senders.shape[2]
    base = pl.multiple_of((shift // 8) * 8, 8)
    rest = shift % 8
    rows = senders[block, pl.ds(base, BLK + 8), :].reshape(BLK // 8 + 1, 8, width)
    turned = pltpu.roll(rows, (8 - rest) % 8, 1)
    place = lax.broadcasted_iota(jnp.int32, (1, 8, width), 1)
    return jnp.where(place < 8 - rest, turned[:-1], turned[1:]).reshape(BLK, width)


RIDERS = 16
SECOND = 2


def call(kernel, out_shape, args, spaces, scratch=(), flops=0, **kwargs):
    specs = [pl.BlockSpec(memory_space=x) for x in spaces]
    args = [pltpu.with_memory_space_constraint(x, at) if at == pltpu.HBM else x for x, at in zip(args, spaces)]
    outs = jax.tree.map(lambda _: pl.BlockSpec(memory_space=pltpu.VMEM), out_shape)
    return pl.pallas_call(
        functools.partial(kernel, **kwargs),
        out_shape=out_shape,
        in_specs=specs,
        out_specs=outs,
        scratch_shapes=list(scratch),
        cost_estimate=pl.CostEstimate(flops=flops, bytes_accessed=1 << 20, transcendentals=0),
        compiler_params=pltpu.CompilerParams(vmem_limit_bytes=32 << 20),
    )(*args)


def parcel_kernel(members, blocks, shifts, parcel, lists, words, sems):
    slots = blocks.shape[1]
    copies = [
        pltpu.make_async_copy(blocks, words.at[pl.ds(0, 1), :], sems.at[0]),
        pltpu.make_async_copy(shifts, words.at[pl.ds(8, 1), :], sems.at[1]),
        pltpu.make_async_copy(members, parcel.at[pl.ds(0, BLK), :], sems.at[2]),
    ]
    for copy in copies:
        copy.start()
    lists[...] = jnp.zeros_like(lists)
    copies[0].wait()
    copies[1].wait()
    lists[0:1, 0:slots] = words[0:1].astype(F32)
    lists[8:9, 0:slots] = words[8:9].astype(F32)
    parcel[BLK:] = lists[...].astype(BF16)
    copies[2].wait()


def addends(values):
    rows, rest = [], values
    for _ in range(3):
        head = rest.astype(BF16).astype(F32)
        rows.append(head)
        rest = rest - head
    rows.append(jnp.zeros_like(rest))
    return jnp.concatenate(rows, axis=0).astype(BF16)


def half_kernel(core, mats, biases, gains, half, terms, sems):
    part = half.shape[0] - RIDERS
    at = pl.multiple_of(core[0] * part, BLK)
    copies = [
        pltpu.make_async_copy(biases, terms.at[pl.ds(0, 2), :], sems.at[0]),
        pltpu.make_async_copy(gains, terms.at[pl.ds(2, 2), :], sems.at[1]),
        pltpu.make_async_copy(mats.at[pl.ds(at, part), :], half.at[pl.ds(0, part), :], sems.at[2]),
    ]
    for copy in copies:
        copy.start()
    copies[0].wait()
    copies[1].wait()
    half[part:] = addends(terms[...])
    copies[2].wait()


def layers_kernel(*refs, where, **kwargs):
    pl.when(refs[0][2] == where)(lambda: whole_member(*refs, **kwargs))


def whole_member(*refs, slots, fresh, given, split):
    place = refs[0]
    refs = refs[1:]
    count = 4 if fresh else 1
    inputs, refs = refs[:count], refs[count:]
    mats, biases, gains = refs[:3]
    refs = refs[3:]
    if given:
        parts, refs = refs[:2], refs[2:]
    outs, refs = (refs[:4], refs[4:]) if split else (refs[:1], refs[1:])
    loaded, own_terms, riders, senders, hidden, words, table, sems = refs[:8]
    width = senders.shape[2]
    nodes = 4 * BLK
    d, e = place[0], place[1]
    part = MATS * width // 4
    half = 2 * part
    plans = [
        [
            pltpu.make_async_copy(biases, own_terms.at[pl.ds(0, 2), :], sems.at[14]),
            pltpu.make_async_copy(gains, own_terms.at[pl.ds(2, 2), :], sems.at[15]),
        ]
        + [
            pltpu.make_async_copy(mats.at[pl.ds(i * width, width), :], loaded.at[0, pl.ds(i * width, width), :], sems.at[i])
            for i in range(MATS)
        ]
    ]
    if given:
        plans.append(
            [
                pltpu.make_async_copy(
                    x.at[pl.ds(0, half), :],
                    loaded.at[1, pl.ds(pl.multiple_of(row * half, BLK), half), :],
                    sems.at[6 + i],
                )
                for i, (x, row) in enumerate(zip(parts, (e, 1 - e)))
            ]
            + [pltpu.make_async_copy(parts[0].at[pl.ds(half, RIDERS), :], riders, sems.at[8])]
        )
    for copies in plans:
        for copy in copies:
            copy.start()

    if fresh:
        copies = [pltpu.make_async_copy(x, refs[8].at[r], sems.at[10 + r]) for r, x in enumerate(inputs)]
        for copy in copies:
            copy.start()
        for copy in copies:
            copy.wait()
        inputs = [refs[8].at[r] for r in range(4)]
        state = jnp.concatenate([x[0:BLK] for x in inputs], axis=0)
        rows = []
        for r in range(4):
            lists = inputs[r][BLK : BLK + 16].astype(F32).astype(jnp.int32)[:, 0:128]
            sender = ((d ^ r) + lists[0:1] + (4 - HB)) % 4 ^ d
            rows += [sender, lists[8:9]]
        numbers = jnp.concatenate(rows, axis=0)
    else:
        state = inputs[0][0:nodes]
        numbers = inputs[0][nodes:].astype(F32).astype(jnp.int32)[0:8, 0:128]
    words[...] = numbers
    to_scalars = pltpu.make_async_copy(words, table, sems.at[9])
    to_scalars.start()

    for at, copies in enumerate(plans):
        last_layer = at == len(plans) - 1
        if at == 0:
            copies[0].wait()
            copies[1].wait()
            terms = own_terms[...]
            matrix_copies = copies[2:]
        else:
            for copy in copies:
                copy.wait()
            values = riders[...].astype(F32)
            terms = values[0:4] + values[4:8] + values[8:12]
            matrix_copies = None

        def mat(i):
            if matrix_copies and matrix_copies[i] is not None:
                matrix_copies[i].wait()
                matrix_copies[i] = None
            return loaded[at, i * width : (i + 1) * width, :]

        sent = dot(state, mat(0)).astype(BF16).astype(F32)
        for b in range(4):
            block = sent[b * BLK : (b + 1) * BLK]
            senders[b, 0:BLK] = block
            senders[b, BLK : 2 * BLK] = block
        received = (dot(state, mat(1)) + terms[0:1]).astype(BF16)
        if at == 0:
            to_scalars.wait()
        collected = []
        for b in range(4):
            for k in range(slots):
                v = shifted_block(senders, table[2 * b, k], table[2 * b + 1, k]).astype(BF16)
                hidden[b, k * BLK : (k + 1) * BLK] = silu(v + received[b * BLK : (b + 1) * BLK])
            edge = dot(hidden[b], mat(2))
            total = norm(edge[0:BLK])
            for k in range(1, slots):
                total += norm(edge[k * BLK : (k + 1) * BLK])
            collected.append((total * terms[2:3]).astype(BF16))
        messages = jnp.concatenate(collected, axis=0)
        pre = dot(state, mat(3)) + dot(messages, mat(4)) + terms[1:2]
        node_out = dot(silu(pre).astype(BF16), mat(5))
        state = (state.astype(F32) + norm(node_out) * terms[3:4]).astype(BF16)
        if last_layer and split:
            for b in range(4):
                outs[b][...] = state[b * BLK : (b + 1) * BLK]
        elif last_layer:
            outs[0][0:nodes] = state
            spare = jnp.zeros((16 - 8, 128), F32)
            outs[0][nodes:, 0:128] = jnp.concatenate([numbers.astype(F32), spare], axis=0).astype(BF16)
            outs[0][nodes:, 128:] = jnp.zeros((16, width - 128), BF16)


def run_layers(place, where, inputs, slots, own, given=None, split=False):
    width = inputs[0].shape[1]
    smem, vmem, hbm = pltpu.SMEM, pltpu.VMEM, pltpu.HBM
    fresh = len(inputs) == 4
    args, spaces = [place] + inputs + list(own), [smem] + [pl.ANY if fresh else vmem] * len(inputs) + [hbm] * 3
    if given:
        args, spaces = args + list(given), spaces + [pl.ANY] * 2
    layers = 1 if given is None else 2
    block = jax.ShapeDtypeStruct((BLK, width), BF16)
    whole = jax.ShapeDtypeStruct((4 * BLK + 16, width), BF16)
    return call(
        layers_kernel,
        [block] * 4 if split else whole,
        args,
        spaces,
        scratch=[
            pltpu.VMEM((layers, MATS * width, width), BF16),
            pltpu.VMEM((4, width), F32),
            pltpu.VMEM((RIDERS, width), BF16),
            pltpu.VMEM((4, 2 * BLK + 8, width), F32),
            pltpu.VMEM((4, slots * BLK, width), BF16),
            pltpu.VMEM((8, 128), jnp.int32),
            pltpu.SMEM((8, 128), jnp.int32),
            pltpu.SemaphoreType.DMA((16,)),
        ]
        + [pltpu.VMEM((4, BLK + 16, width), BF16)] * fresh,
        flops=layers * 2 * 4 * BLK * (slots + 5) * width * width,
        where=where,
        slots=slots,
        fresh=fresh,
        given=given is not None,
        split=split,
    )


def messages_kernel(place, *refs, targets):
    blocks, refs = refs[:4], refs[4:]
    outs, held = refs[:-1], refs[-1]
    total = jnp.zeros(blocks[0].shape, F32)
    for r, block in enumerate(blocks):
        held[r] = block[...]
        total += block[...].astype(F32)
    for out, section in zip(outs, targets):
        out[0:BLK] = held[place[0] ^ section]
        out[BLK:] = total.astype(BF16)


def in_two_stages(members, layer_mats, biases, norm_gains, edge_blocks, edge_shift):
    doms, cores = lax.axis_size("dom"), lax.axis_size("ens")
    layers = lax.axis_size("section")
    s, d, e = (lax.axis_index(a) for a in AXES)
    slots = edge_blocks.shape[1]
    width = members.shape[2]
    mats = layer_mats[0].reshape(MATS * width, width)
    part = MATS * width // 4
    place = jnp.stack([d, e, s]).astype(jnp.int32)
    smem, vmem = pltpu.SMEM, pltpu.VMEM
    spots = [(i, j, k) for i in range(layers) for j in range(doms) for k in range(cores)]

    def shape(rows):
        return jax.ShapeDtypeStruct((rows, width), BF16)

    def index(i, j, k):
        return (i * doms + j) * cores + k

    def send(x, pairs):
        return lax.ppermute(x, AXES, [(index(*a), index(*b)) for a, b in pairs])

    def swap(x, by):
        a, b, c = by
        return send(x, [((i, j, k), (i ^ a, j ^ b, k ^ c)) for i, j, k in spots])

    def hop(x, source, target):
        return send(x, [((source, j, k), (target, j, k)) for i, j, k in spots if i == source])

    hbm = pltpu.HBM
    parcel = call(
        parcel_kernel,
        shape(BLK + 16),
        (members[0], edge_blocks, edge_shift),
        [hbm] * 3,
        [pltpu.VMEM((16, width), F32), pltpu.VMEM((16, slots), jnp.int32), pltpu.SemaphoreType.DMA((3,))],
    )
    arrived = [
        send(parcel, [((i, i ^ r, k), (0, i, k)) for i in range(layers) for k in range(cores)])
        for r in range(doms)
    ]

    own = (mats, biases[0], norm_gains[0])
    half = call(
        half_kernel,
        shape(2 * part + RIDERS),
        (place[1:2], *own),
        [smem] + [hbm] * 3,
        [pltpu.VMEM((4, width), F32), pltpu.SemaphoreType.DMA((3,))],
    )
    half = hop(half, layers - 1, SECOND)

    state = run_layers(place, 0, arrived, slots, own)
    state = hop(state, 0, 1)
    state = run_layers(place, 1, [state], slots, own)
    half = lax.optimization_barrier((half, state))[0]
    given = (half, swap(half, (0, 0, 1)))
    state = hop(state, 1, SECOND)
    blocks = run_layers(place, SECOND, [state], slots, own, given, split=True)

    columns = [blocks[0]] + [swap(blocks[r], (0, r, 0)) for r in range(1, doms)]
    targets = [i for i in range(layers) if i != SECOND] + [SECOND]
    packed = call(
        messages_kernel,
        [shape(2 * BLK)] * layers,
        (place, *columns),
        [smem] + [vmem] * doms,
        [pltpu.VMEM((doms, BLK, width), BF16)],
        targets=targets,
    )
    final = packed[-1]
    for i, message in zip(targets[:-1], packed):
        final = jnp.where(s == i, hop(message, SECOND, i), final)
    total = final[BLK:]
    total = total.astype(F32) + swap(total, (0, 0, 1)).astype(F32)
    count = members.shape[0] * layers * cores
    return (final[None, :BLK], total / count)


def solution(mesh):
    shape = dict(mesh.shape)
    placed = (
        P(("section", "ens"), "dom", None),
        P("section", None, None, None),
        P("section", None, None),
        P("section", None, None),
        P("dom", None),
        P("dom", None),
    )

    def on_device(members, layer_mats, biases, norm_gains, edge_blocks, edge_shift):
        small = shape["section"] == 4 and shape["dom"] == 4 and shape["ens"] == 2
        one_each = members.shape[:2] == (1, BLK) and layer_mats.shape[0] == 1
        plan = in_two_stages if small and one_each else in_rounds
        return plan(members, layer_mats, biases, norm_gains, edge_blocks, edge_shift)

    return jax.shard_map(
        on_device,
        mesh=mesh,
        in_specs=placed,
        out_specs=(P(("section", "ens"), "dom", None), P("dom", None)),
        check_vma=False,
    )
```

```python
import functools

import jax
import jax.numpy as jnp
from jax import lax
from jax.experimental import pallas as pl
from jax.experimental.pallas import tpu as pltpu
from jax.sharding import PartitionSpec as P

BLK = 128
HB = 1
EPSILON = 1e-05
MATS = 6
F32 = jnp.float32
BF16 = jnp.bfloat16
AXES = ("section", "dom", "ens")


def with_halo(x, sides, width):
    for axis, dim in sides:
        devices, length = (lax.axis_size(axis), x.shape[dim])
        up = [(i, (i + 1) % devices) for i in range(devices)]
        down = [(j, i) for i, j in up]
        last = lax.slice_in_dim(x, length - width, length, axis=dim)
        first = lax.slice_in_dim(x, 0, width, axis=dim)
        before = lax.ppermute(last, axis, up)
        after = lax.ppermute(first, axis, down)
        x = jnp.concatenate([before, x, after], axis=dim)
    return x


def from_behind(x, axis, by):
    devices = lax.axis_size(axis)
    return lax.ppermute(x, axis, [(i, (i + by) % devices) for i in range(devices)])


def layer_norm(values):
    average = jnp.mean(values, axis=-1, keepdims=True)
    centred = values - average
    spread = jnp.mean(centred * centred, axis=-1, keepdims=True)
    return centred * lax.rsqrt(spread + EPSILON)


def project(values, weight):
    return jnp.einsum("mnd,de->mne", values, weight, preferred_element_type=jnp.float32)


def fetch_rim(state, send_weight):
    outgoing = project(state, send_weight).astype(jnp.bfloat16)
    extended = with_halo(outgoing, (("dom", 1),), HB * BLK)
    return extended


def update_nodes(state, sender_terms, sender_rows, matrices, bias_pair, gain_pair):
    batch_size, node_count, width_d = state.shape
    slot_count = sender_rows.shape[1]
    receiver_terms = project(state, matrices[1]) + bias_pair[0]
    picked = jnp.take(sender_terms, sender_rows.reshape(-1), axis=1).reshape(
        batch_size, node_count, slot_count, width_d
    )
    pre_act = picked.astype(jnp.float32) + receiver_terms[:, :, None, :]
    hidden = jax.nn.silu(pre_act).astype(jnp.bfloat16)
    edge_out = jnp.einsum("mnkd,de->mnke", hidden, matrices[2], preferred_element_type=jnp.float32)
    messages = jnp.sum(layer_norm(edge_out) * gain_pair[0], axis=2).astype(jnp.bfloat16)
    node_pre = project(state, matrices[3]) + project(messages, matrices[4]) + bias_pair[1]
    node_hidden = jax.nn.silu(node_pre).astype(jnp.bfloat16)
    node_out = project(node_hidden, matrices[5])
    return (state.astype(jnp.float32) + layer_norm(node_out) * gain_pair[1]).astype(jnp.bfloat16)


def in_rounds(members, layer_mats, biases, norm_gains, edge_blocks, edge_shift):
    blocks = edge_blocks.shape[0]
    block_rows = jnp.repeat(edge_blocks, BLK, axis=0)
    row_offsets = jnp.repeat(edge_shift, BLK, axis=0)
    positions = (jnp.arange(blocks * BLK, dtype=jnp.int32) % BLK)[:, None]
    sender_rows = block_rows * BLK + (positions + row_offsets) % BLK
    sections = lax.axis_size("section")
    section_index = lax.axis_index("section")
    matrices = layer_mats[0]
    bias_pair = biases[0]
    gain_pair = norm_gains[0]

    def advance(moment, state):
        anchor = (section_index - moment) % sections
        entry_tick = (sections - anchor) % sections
        active = jnp.logical_and(moment >= entry_tick, moment - entry_tick < sections)
        sender_terms = fetch_rim(state, matrices[0])
        state = lax.cond(
            active,
            lambda: update_nodes(state, sender_terms, sender_rows, matrices, bias_pair, gain_pair),
            lambda: state,
        )
        return from_behind(state, "section", 1)

    final_state = lax.fori_loop(0, 2 * sections, advance, members)
    member_count = final_state.shape[0] * sections * lax.axis_size("ens")
    member_total = lax.psum(
        jnp.sum(final_state.astype(jnp.float32), axis=0).astype(jnp.bfloat16), ("section", "ens")
    ).astype(jnp.float32)
    return (final_state, member_total / member_count)


def silu(v):
    half = jnp.asarray(0.5, v.dtype) * v
    return half + half * jnp.tanh(half)


def norm(v):
    scale = 1.0 / v.shape[-1]
    centred = v - jnp.sum(v, axis=-1, keepdims=True) * scale
    spread = jnp.sum(centred * centred, axis=-1, keepdims=True) * scale
    return centred * lax.rsqrt(spread + EPSILON)


def dot(a, b):
    return jnp.dot(a, b, preferred_element_type=F32)


def shifted_block(senders, block, shift):
    width = senders.shape[2]
    base = pl.multiple_of((shift // 8) * 8, 8)
    rest = shift % 8
    rows = senders[block, pl.ds(base, BLK + 8), :].reshape(BLK // 8 + 1, 8, width)
    turned = pltpu.roll(rows, (8 - rest) % 8, 1)
    place = lax.broadcasted_iota(jnp.int32, (1, 8, width), 1)
    return jnp.where(place < 8 - rest, turned[:-1], turned[1:]).reshape(BLK, width)


RIDERS = 16
SECOND = 2


def call(kernel, out_shape, args, spaces, scratch=(), flops=0, **kwargs):
    specs = [pl.BlockSpec(memory_space=x) for x in spaces]
    args = [pltpu.with_memory_space_constraint(x, at) if at == pltpu.HBM else x for x, at in zip(args, spaces)]
    outs = jax.tree.map(lambda _: pl.BlockSpec(memory_space=pltpu.VMEM), out_shape)
    return pl.pallas_call(
        functools.partial(kernel, **kwargs),
        out_shape=out_shape,
        in_specs=specs,
        out_specs=outs,
        scratch_shapes=list(scratch),
        cost_estimate=pl.CostEstimate(flops=flops, bytes_accessed=1 << 20, transcendentals=0),
        compiler_params=pltpu.CompilerParams(vmem_limit_bytes=32 << 20),
    )(*args)


def parcel_kernel(members, blocks, shifts, parcel, lists, words, sems):
    slots = blocks.shape[1]
    copies = [
        pltpu.make_async_copy(blocks, words.at[pl.ds(0, 1), :], sems.at[0]),
        pltpu.make_async_copy(shifts, words.at[pl.ds(8, 1), :], sems.at[1]),
        pltpu.make_async_copy(members, parcel.at[pl.ds(0, BLK), :], sems.at[2]),
    ]
    for copy in copies:
        copy.start()
    lists[...] = jnp.zeros_like(lists)
    copies[0].wait()
    copies[1].wait()
    lists[0:1, 0:slots] = words[0:1].astype(F32)
    lists[8:9, 0:slots] = words[8:9].astype(F32)
    parcel[BLK:] = lists[...].astype(BF16)
    copies[2].wait()


def addends(values):
    rows, rest = [], values
    for _ in range(3):
        head = rest.astype(BF16).astype(F32)
        rows.append(head)
        rest = rest - head
    rows.append(jnp.zeros_like(rest))
    return jnp.concatenate(rows, axis=0).astype(BF16)


def half_kernel(core, mats, biases, gains, half, terms, sems):
    part = half.shape[0] - RIDERS
    at = pl.multiple_of(core[0] * part, BLK)
    copies = [
        pltpu.make_async_copy(biases, terms.at[pl.ds(0, 2), :], sems.at[0]),
        pltpu.make_async_copy(gains, terms.at[pl.ds(2, 2), :], sems.at[1]),
        pltpu.make_async_copy(mats.at[pl.ds(at, part), :], half.at[pl.ds(0, part), :], sems.at[2]),
    ]
    for copy in copies:
        copy.start()
    copies[0].wait()
    copies[1].wait()
    half[part:] = addends(terms[...])
    copies[2].wait()


def layers_kernel(*refs, where, **kwargs):
    pl.when(refs[0][2] == where)(lambda: whole_member(*refs, **kwargs))


def whole_member(*refs, slots, fresh, given, split):
    place = refs[0]
    refs = refs[1:]
    count = 4 if fresh else 1
    inputs, refs = refs[:count], refs[count:]
    mats, biases, gains = refs[:3]
    refs = refs[3:]
    if given:
        parts, refs = refs[:2], refs[2:]
    outs, refs = (refs[:4], refs[4:]) if split else (refs[:1], refs[1:])
    loaded, riders, senders, hidden, words, table, sems = refs[:7]
    width = senders.shape[2]
    nodes = 4 * BLK
    d, e = place[0], place[1]
    part = MATS * width // 4
    half = 2 * part
    plans = [[]]
    if given:
        plans.append(
            [
                pltpu.make_async_copy(
                    x.at[pl.ds(0, half), :],
                    loaded.at[pl.ds(pl.multiple_of(row * half, BLK), half), :],
                    sems.at[6 + i],
                )
                for i, (x, row) in enumerate(zip(parts, (e, 1 - e)))
            ]
            + [pltpu.make_async_copy(parts[0].at[pl.ds(half, RIDERS), :], riders, sems.at[8])]
        )
    for copies in plans:
        for copy in copies:
            copy.start()

    if fresh:
        copies = [pltpu.make_async_copy(x, refs[7].at[r], sems.at[10 + r]) for r, x in enumerate(inputs)]
        for copy in copies:
            copy.start()
        for copy in copies:
            copy.wait()
        inputs = [refs[7].at[r] for r in range(4)]
        state = jnp.concatenate([x[0:BLK] for x in inputs], axis=0)
        rows = []
        for r in range(4):
            lists = inputs[r][BLK : BLK + 16].astype(F32).astype(jnp.int32)[:, 0:128]
            sender = ((d ^ r) + lists[0:1] + (4 - HB)) % 4 ^ d
            rows += [sender, lists[8:9]]
        numbers = jnp.concatenate(rows, axis=0)
    else:
        state = inputs[0][0:nodes]
        numbers = inputs[0][nodes:].astype(F32).astype(jnp.int32)[0:8, 0:128]
    words[...] = numbers
    to_scalars = pltpu.make_async_copy(words, table, sems.at[9])
    to_scalars.start()

    for at, copies in enumerate(plans):
        last_layer = at == len(plans) - 1
        if at == 0:
            terms = jnp.concatenate([biases[...], gains[...]], axis=0)
            source = mats
        else:
            for copy in copies:
                copy.wait()
            values = riders[...].astype(F32)
            terms = values[0:4] + values[4:8] + values[8:12]
            source = loaded

        def mat(i):
            return source[i * width : (i + 1) * width, :]

        sent = dot(state, mat(0)).astype(BF16).astype(F32)
        for b in range(4):
            block = sent[b * BLK : (b + 1) * BLK]
            senders[b, 0:BLK] = block
            senders[b, BLK : 2 * BLK] = block
        received = (dot(state, mat(1)) + terms[0:1]).astype(BF16)
        if at == 0:
            to_scalars.wait()
        collected = []
        for b in range(4):
            for k in range(slots):
                v = shifted_block(senders, table[2 * b, k], table[2 * b + 1, k]).astype(BF16)
                hidden[b, k * BLK : (k + 1) * BLK] = silu(v + received[b * BLK : (b + 1) * BLK])
            edge = dot(hidden[b], mat(2))
            total = norm(edge[0:BLK])
            for k in range(1, slots):
                total += norm(edge[k * BLK : (k + 1) * BLK])
            collected.append((total * terms[2:3]).astype(BF16))
        messages = jnp.concatenate(collected, axis=0)
        pre = dot(state, mat(3)) + dot(messages, mat(4)) + terms[1:2]
        node_out = dot(silu(pre).astype(BF16), mat(5))
        state = (state.astype(F32) + norm(node_out) * terms[3:4]).astype(BF16)
        if last_layer and split:
            for b in range(4):
                outs[b][...] = state[b * BLK : (b + 1) * BLK]
        elif last_layer:
            outs[0][0:nodes] = state
            spare = jnp.zeros((16 - 8, 128), F32)
            outs[0][nodes:, 0:128] = jnp.concatenate([numbers.astype(F32), spare], axis=0).astype(BF16)
            outs[0][nodes:, 128:] = jnp.zeros((16, width - 128), BF16)


def run_layers(place, where, inputs, slots, own, given=None, split=False):
    width = inputs[0].shape[1]
    smem, vmem = pltpu.SMEM, pltpu.VMEM
    fresh = len(inputs) == 4
    args, spaces = [place] + inputs + list(own), [smem] + [pl.ANY if fresh else vmem] * len(inputs) + [vmem] * 3
    if given:
        args, spaces = args + list(given), spaces + [pl.ANY] * 2
    layers = 1 if given is None else 2
    block = jax.ShapeDtypeStruct((BLK, width), BF16)
    whole = jax.ShapeDtypeStruct((4 * BLK + 16, width), BF16)
    return call(
        layers_kernel,
        [block] * 4 if split else whole,
        args,
        spaces,
        scratch=[
            pltpu.VMEM((MATS * width if given else 16, width), BF16),
            pltpu.VMEM((RIDERS, width), BF16),
            pltpu.VMEM((4, 2 * BLK + 8, width), F32),
            pltpu.VMEM((4, slots * BLK, width), BF16),
            pltpu.VMEM((8, 128), jnp.int32),
            pltpu.SMEM((8, 128), jnp.int32),
            pltpu.SemaphoreType.DMA((16,)),
        ]
        + [pltpu.VMEM((4, BLK + 16, width), BF16)] * fresh,
        flops=layers * 2 * 4 * BLK * (slots + 5) * width * width,
        where=where,
        slots=slots,
        fresh=fresh,
        given=given is not None,
        split=split,
    )


def messages_kernel(place, *refs, targets):
    blocks, refs = refs[:4], refs[4:]
    outs, held = refs[:-1], refs[-1]
    total = jnp.zeros(blocks[0].shape, F32)
    for r, block in enumerate(blocks):
        held[r] = block[...]
        total += block[...].astype(F32)
    for out, section in zip(outs, targets):
        out[0:BLK] = held[place[0] ^ section]
        out[BLK:] = total.astype(BF16)


def in_two_stages(members, layer_mats, biases, norm_gains, edge_blocks, edge_shift):
    doms, cores = lax.axis_size("dom"), lax.axis_size("ens")
    layers = lax.axis_size("section")
    s, d, e = (lax.axis_index(a) for a in AXES)
    slots = edge_blocks.shape[1]
    width = members.shape[2]
    mats = layer_mats[0].reshape(MATS * width, width)
    part = MATS * width // 4
    place = jnp.stack([d, e, s]).astype(jnp.int32)
    smem, vmem = pltpu.SMEM, pltpu.VMEM
    spots = [(i, j, k) for i in range(layers) for j in range(doms) for k in range(cores)]

    def shape(rows):
        return jax.ShapeDtypeStruct((rows, width), BF16)

    def index(i, j, k):
        return (i * doms + j) * cores + k

    def send(x, pairs):
        return lax.ppermute(x, AXES, [(index(*a), index(*b)) for a, b in pairs])

    def swap(x, by):
        a, b, c = by
        return send(x, [((i, j, k), (i ^ a, j ^ b, k ^ c)) for i, j, k in spots])

    def hop(x, source, target):
        return send(x, [((source, j, k), (target, j, k)) for i, j, k in spots if i == source])

    hbm = pltpu.HBM
    parcel = call(
        parcel_kernel,
        shape(BLK + 16),
        (members[0], edge_blocks, edge_shift),
        [hbm] * 3,
        [pltpu.VMEM((16, width), F32), pltpu.VMEM((16, slots), jnp.int32), pltpu.SemaphoreType.DMA((3,))],
    )
    arrived = [
        send(parcel, [((i, i ^ r, k), (0, i, k)) for i in range(layers) for k in range(cores)])
        for r in range(doms)
    ]

    own = (mats, biases[0], norm_gains[0])
    half = call(
        half_kernel,
        shape(2 * part + RIDERS),
        (place[1:2], *own),
        [smem] + [hbm] * 3,
        [pltpu.VMEM((4, width), F32), pltpu.SemaphoreType.DMA((3,))],
    )
    half = hop(half, layers - 1, SECOND)

    state = run_layers(place, 0, arrived, slots, own)
    state = hop(state, 0, 1)
    state = run_layers(place, 1, [state], slots, own)
    half = lax.optimization_barrier((half, state))[0]
    given = (half, swap(half, (0, 0, 1)))
    state = hop(state, 1, SECOND)
    blocks = run_layers(place, SECOND, [state], slots, own, given, split=True)

    columns = [blocks[0]] + [swap(blocks[r], (0, r, 0)) for r in range(1, doms)]
    targets = [i for i in range(layers) if i != SECOND] + [SECOND]
    packed = call(
        messages_kernel,
        [shape(2 * BLK)] * layers,
        (place, *columns),
        [smem] + [vmem] * doms,
        [pltpu.VMEM((doms, BLK, width), BF16)],
        targets=targets,
    )
    final = packed[-1]
    for i, message in zip(targets[:-1], packed):
        final = jnp.where(s == i, hop(message, SECOND, i), final)
    total = final[BLK:]
    total = total.astype(F32) + swap(total, (0, 0, 1)).astype(F32)
    count = members.shape[0] * layers * cores
    return (final[None, :BLK], total / count)


def solution(mesh):
    shape = dict(mesh.shape)
    placed = (
        P(("section", "ens"), "dom", None),
        P("section", None, None, None),
        P("section", None, None),
        P("section", None, None),
        P("dom", None),
        P("dom", None),
    )

    def on_device(members, layer_mats, biases, norm_gains, edge_blocks, edge_shift):
        small = shape["section"] == 4 and shape["dom"] == 4 and shape["ens"] == 2
        one_each = members.shape[:2] == (1, BLK) and layer_mats.shape[0] == 1
        plan = in_two_stages if small and one_each else in_rounds
        return plan(members, layer_mats, biases, norm_gains, edge_blocks, edge_shift)

    return jax.shard_map(
        on_device,
        mesh=mesh,
        in_specs=placed,
        out_specs=(P(("section", "ens"), "dom", None), P("dom", None)),
        check_vma=False,
    )
```

```python
import functools

import jax
import jax.numpy as jnp
from jax import lax
from jax.experimental import pallas as pl
from jax.experimental.pallas import tpu as pltpu
from jax.sharding import PartitionSpec as P

BLK = 128
HB = 1
EPSILON = 1e-05
MATS = 6
F32 = jnp.float32
BF16 = jnp.bfloat16
AXES = ("section", "dom", "ens")


def with_halo(x, sides, width):
    for axis, dim in sides:
        devices, length = (lax.axis_size(axis), x.shape[dim])
        up = [(i, (i + 1) % devices) for i in range(devices)]
        down = [(j, i) for i, j in up]
        last = lax.slice_in_dim(x, length - width, length, axis=dim)
        first = lax.slice_in_dim(x, 0, width, axis=dim)
        before = lax.ppermute(last, axis, up)
        after = lax.ppermute(first, axis, down)
        x = jnp.concatenate([before, x, after], axis=dim)
    return x


def from_behind(x, axis, by):
    devices = lax.axis_size(axis)
    return lax.ppermute(x, axis, [(i, (i + by) % devices) for i in range(devices)])


def layer_norm(values):
    average = jnp.mean(values, axis=-1, keepdims=True)
    centred = values - average
    spread = jnp.mean(centred * centred, axis=-1, keepdims=True)
    return centred * lax.rsqrt(spread + EPSILON)


def project(values, weight):
    return jnp.einsum("mnd,de->mne", values, weight, preferred_element_type=jnp.float32)


def fetch_rim(state, send_weight):
    outgoing = project(state, send_weight).astype(jnp.bfloat16)
    extended = with_halo(outgoing, (("dom", 1),), HB * BLK)
    return extended


def update_nodes(state, sender_terms, sender_rows, matrices, bias_pair, gain_pair):
    batch_size, node_count, width_d = state.shape
    slot_count = sender_rows.shape[1]
    receiver_terms = project(state, matrices[1]) + bias_pair[0]
    picked = jnp.take(sender_terms, sender_rows.reshape(-1), axis=1).reshape(
        batch_size, node_count, slot_count, width_d
    )
    pre_act = picked.astype(jnp.float32) + receiver_terms[:, :, None, :]
    hidden = jax.nn.silu(pre_act).astype(jnp.bfloat16)
    edge_out = jnp.einsum("mnkd,de->mnke", hidden, matrices[2], preferred_element_type=jnp.float32)
    messages = jnp.sum(layer_norm(edge_out) * gain_pair[0], axis=2).astype(jnp.bfloat16)
    node_pre = project(state, matrices[3]) + project(messages, matrices[4]) + bias_pair[1]
    node_hidden = jax.nn.silu(node_pre).astype(jnp.bfloat16)
    node_out = project(node_hidden, matrices[5])
    return (state.astype(jnp.float32) + layer_norm(node_out) * gain_pair[1]).astype(jnp.bfloat16)


def in_rounds(members, layer_mats, biases, norm_gains, edge_blocks, edge_shift):
    blocks = edge_blocks.shape[0]
    block_rows = jnp.repeat(edge_blocks, BLK, axis=0)
    row_offsets = jnp.repeat(edge_shift, BLK, axis=0)
    positions = (jnp.arange(blocks * BLK, dtype=jnp.int32) % BLK)[:, None]
    sender_rows = block_rows * BLK + (positions + row_offsets) % BLK
    sections = lax.axis_size("section")
    section_index = lax.axis_index("section")
    matrices = layer_mats[0]
    bias_pair = biases[0]
    gain_pair = norm_gains[0]

    def advance(moment, state):
        anchor = (section_index - moment) % sections
        entry_tick = (sections - anchor) % sections
        active = jnp.logical_and(moment >= entry_tick, moment - entry_tick < sections)
        sender_terms = fetch_rim(state, matrices[0])
        state = lax.cond(
            active,
            lambda: update_nodes(state, sender_terms, sender_rows, matrices, bias_pair, gain_pair),
            lambda: state,
        )
        return from_behind(state, "section", 1)

    final_state = lax.fori_loop(0, 2 * sections, advance, members)
    member_count = final_state.shape[0] * sections * lax.axis_size("ens")
    member_total = lax.psum(
        jnp.sum(final_state.astype(jnp.float32), axis=0).astype(jnp.bfloat16), ("section", "ens")
    ).astype(jnp.float32)
    return (final_state, member_total / member_count)


def silu(v):
    half = jnp.asarray(0.5, v.dtype) * v
    return half + half * jnp.tanh(half)


def norm(v):
    scale = 1.0 / v.shape[-1]
    centred = v - jnp.sum(v, axis=-1, keepdims=True) * scale
    spread = jnp.sum(centred * centred, axis=-1, keepdims=True) * scale
    return centred * lax.rsqrt(spread + EPSILON)


def dot(a, b):
    return jnp.dot(a, b, preferred_element_type=F32)


def shifted_block(senders, block, shift):
    width = senders.shape[2]
    base = pl.multiple_of((shift // 8) * 8, 8)
    rest = shift % 8
    rows = senders[block, pl.ds(base, BLK + 8), :].reshape(BLK // 8 + 1, 8, width)
    turned = pltpu.roll(rows, (8 - rest) % 8, 1)
    place = lax.broadcasted_iota(jnp.int32, (1, 8, width), 1)
    return jnp.where(place < 8 - rest, turned[:-1], turned[1:]).reshape(BLK, width)


RIDERS = 16
SECOND = 2


def call(kernel, out_shape, args, spaces, scratch=(), flops=0, **kwargs):
    specs = [pl.BlockSpec(memory_space=x) for x in spaces]
    args = [pltpu.with_memory_space_constraint(x, at) if at == pltpu.HBM else x for x, at in zip(args, spaces)]
    outs = jax.tree.map(lambda _: pl.BlockSpec(memory_space=pltpu.VMEM), out_shape)
    return pl.pallas_call(
        functools.partial(kernel, **kwargs),
        out_shape=out_shape,
        in_specs=specs,
        out_specs=outs,
        scratch_shapes=list(scratch),
        cost_estimate=pl.CostEstimate(flops=flops, bytes_accessed=1 << 20, transcendentals=0),
        compiler_params=pltpu.CompilerParams(vmem_limit_bytes=32 << 20),
    )(*args)


def parcel_kernel(members, blocks, shifts, parcel, lists, words, sems):
    slots = blocks.shape[1]
    copies = [
        pltpu.make_async_copy(blocks, words.at[pl.ds(0, 1), :], sems.at[0]),
        pltpu.make_async_copy(shifts, words.at[pl.ds(8, 1), :], sems.at[1]),
        pltpu.make_async_copy(members, parcel.at[pl.ds(0, BLK), :], sems.at[2]),
    ]
    for copy in copies:
        copy.start()
    lists[...] = jnp.zeros_like(lists)
    copies[0].wait()
    copies[1].wait()
    lists[0:1, 0:slots] = words[0:1].astype(F32)
    lists[8:9, 0:slots] = words[8:9].astype(F32)
    parcel[BLK:] = lists[...].astype(BF16)
    copies[2].wait()


def addends(values):
    rows, rest = [], values
    for _ in range(3):
        head = rest.astype(BF16).astype(F32)
        rows.append(head)
        rest = rest - head
    rows.append(jnp.zeros_like(rest))
    return jnp.concatenate(rows, axis=0).astype(BF16)


def half_kernel(core, mats, biases, gains, half, terms, sems):
    part = half.shape[0] - RIDERS
    at = pl.multiple_of(core[0] * part, BLK)
    copies = [
        pltpu.make_async_copy(biases, terms.at[pl.ds(0, 2), :], sems.at[0]),
        pltpu.make_async_copy(gains, terms.at[pl.ds(2, 2), :], sems.at[1]),
        pltpu.make_async_copy(mats.at[pl.ds(at, part), :], half.at[pl.ds(0, part), :], sems.at[2]),
    ]
    for copy in copies:
        copy.start()
    copies[0].wait()
    copies[1].wait()
    half[part:] = addends(terms[...])
    copies[2].wait()


def layers_kernel(*refs, where, **kwargs):
    pl.when(refs[0][2] == where)(lambda: whole_member(*refs, **kwargs))


def whole_member(*refs, slots, fresh, given, split, chosen):
    place = refs[0]
    refs = refs[1:]
    count = 4 if fresh else 2
    low, high = chosen
    picked = slice(low * BLK, high * BLK)
    inputs, refs = refs[:count], refs[count:]
    mats, biases, gains = refs[:3]
    refs = refs[3:]
    if given:
        parts, refs = refs[:2], refs[2:]
    outs, refs = (refs[:4], refs[4:]) if split else (refs[:1], refs[1:])
    loaded, riders, senders, hidden, words, table, sems = refs[:7]
    width = senders.shape[2]
    d, e = place[0], place[1]
    part = MATS * width // 4
    half = 2 * part
    plans = [[]]
    if given:
        plans.append(
            [
                pltpu.make_async_copy(
                    x.at[pl.ds(0, half), :],
                    loaded.at[pl.ds(pl.multiple_of(row * half, BLK), half), :],
                    sems.at[6 + i],
                )
                for i, (x, row) in enumerate(zip(parts, (e, 1 - e)))
            ]
            + [pltpu.make_async_copy(parts[0].at[pl.ds(half, RIDERS), :], riders, sems.at[8])]
        )
    for copies in plans:
        for copy in copies:
            copy.start()

    if fresh:
        copies = [pltpu.make_async_copy(x, refs[7].at[r], sems.at[10 + r]) for r, x in enumerate(inputs)]
        for copy in copies:
            copy.start()
        for copy in copies:
            copy.wait()
        inputs = [refs[7].at[r] for r in range(4)]
        state = jnp.concatenate([x[0:BLK] for x in inputs], axis=0)
        rows = []
        for r in range(4):
            lists = inputs[r][BLK : BLK + 16].astype(F32).astype(jnp.int32)[:, 0:128]
            sender = ((d ^ r) + lists[0:1] + (4 - HB)) % 4 ^ d
            rows += [sender, lists[8:9]]
        numbers = jnp.concatenate(rows, axis=0)
    else:
        state = jnp.concatenate([x[0 : 2 * BLK] for x in inputs], axis=0)
        numbers = inputs[0][2 * BLK :].astype(F32).astype(jnp.int32)[0:8, 0:128]
    words[...] = numbers
    to_scalars = pltpu.make_async_copy(words, table, sems.at[9])
    to_scalars.start()

    for at, copies in enumerate(plans):
        last_layer = at == len(plans) - 1
        if at == 0:
            terms = jnp.concatenate([biases[...], gains[...]], axis=0)
            source = mats
        else:
            for copy in copies:
                copy.wait()
            values = riders[...].astype(F32)
            terms = values[0:4] + values[4:8] + values[8:12]
            source = loaded

        def mat(i):
            return source[i * width : (i + 1) * width, :]

        sent = dot(state, mat(0)).astype(BF16).astype(F32)
        for b in range(4):
            block = sent[b * BLK : (b + 1) * BLK]
            senders[b, 0:BLK] = block
            senders[b, BLK : 2 * BLK] = block
        state = state[picked]
        received = (dot(state, mat(1)) + terms[0:1]).astype(BF16)
        if at == 0:
            to_scalars.wait()
        collected = []
        for b in range(low, high):
            for k in range(slots):
                v = shifted_block(senders, table[2 * b, k], table[2 * b + 1, k]).astype(BF16)
                hidden[b, k * BLK : (k + 1) * BLK] = silu(v + received[(b - low) * BLK : (b - low + 1) * BLK])
            edge = dot(hidden[b], mat(2))
            total = norm(edge[0:BLK])
            for k in range(1, slots):
                total += norm(edge[k * BLK : (k + 1) * BLK])
            collected.append((total * terms[2:3]).astype(BF16))
        messages = jnp.concatenate(collected, axis=0)
        pre = dot(state, mat(3)) + dot(messages, mat(4)) + terms[1:2]
        node_out = dot(silu(pre.astype(BF16)), mat(5))
        state = (state.astype(F32) + norm(node_out) * terms[3:4]).astype(BF16)
        if last_layer and split:
            for b in range(4):
                outs[b][...] = state[b * BLK : (b + 1) * BLK]
        elif last_layer:
            outs[0][0 : (high - low) * BLK] = state
        if last_layer and not split and low == 0:
            nodes = high * BLK
            spare = jnp.zeros((16 - 8, 128), F32)
            outs[0][nodes:, 0:128] = jnp.concatenate([numbers.astype(F32), spare], axis=0).astype(BF16)
            outs[0][nodes:, 128:] = jnp.zeros((16, width - 128), BF16)


def run_layers(place, where, inputs, slots, own, given=None, split=False, chosen=(0, 4)):
    width = inputs[0].shape[1]
    smem, vmem = pltpu.SMEM, pltpu.VMEM
    fresh = len(inputs) == 4
    args, spaces = [place] + inputs + list(own), [smem] + [pl.ANY if fresh else vmem] * len(inputs) + [vmem] * 3
    if given:
        args, spaces = args + list(given), spaces + [pl.ANY] * 2
    layers = 1 if given is None else 2
    block = jax.ShapeDtypeStruct((BLK, width), BF16)
    low, high = chosen
    whole = jax.ShapeDtypeStruct(((high - low) * BLK + (16 if low == 0 else 0), width), BF16)
    return call(
        layers_kernel,
        [block] * 4 if split else whole,
        args,
        spaces,
        scratch=[
            pltpu.VMEM((MATS * width if given else 16, width), BF16),
            pltpu.VMEM((RIDERS, width), BF16),
            pltpu.VMEM((4, 2 * BLK + 8, width), F32),
            pltpu.VMEM((4, slots * BLK, width), BF16),
            pltpu.VMEM((8, 128), jnp.int32),
            pltpu.SMEM((8, 128), jnp.int32),
            pltpu.SemaphoreType.DMA((16,)),
        ]
        + [pltpu.VMEM((4, BLK + 16, width), BF16)] * fresh,
        flops=layers * 2 * (high - low) * BLK * (slots + 5) * width * width,
        where=where,
        slots=slots,
        fresh=fresh,
        given=given is not None,
        split=split,
        chosen=chosen,
    )


def messages_kernel(place, *refs, targets):
    blocks, refs = refs[:4], refs[4:]
    outs, held = refs[:-1], refs[-1]
    total = jnp.zeros(blocks[0].shape, F32)
    for r, block in enumerate(blocks):
        held[r] = block[...]
        total += block[...].astype(F32)
    for out, section in zip(outs, targets):
        out[0:BLK] = held[place[0] ^ section]
        out[BLK:] = total.astype(BF16)


def in_two_stages(members, layer_mats, biases, norm_gains, edge_blocks, edge_shift):
    doms, cores = lax.axis_size("dom"), lax.axis_size("ens")
    layers = lax.axis_size("section")
    s, d, e = (lax.axis_index(a) for a in AXES)
    slots = edge_blocks.shape[1]
    width = members.shape[2]
    mats = layer_mats[0].reshape(MATS * width, width)
    part = MATS * width // 4
    place = jnp.stack([d, e, s]).astype(jnp.int32)
    smem, vmem = pltpu.SMEM, pltpu.VMEM
    spots = [(i, j, k) for i in range(layers) for j in range(doms) for k in range(cores)]

    def shape(rows):
        return jax.ShapeDtypeStruct((rows, width), BF16)

    def index(i, j, k):
        return (i * doms + j) * cores + k

    def send(x, pairs):
        return lax.ppermute(x, AXES, [(index(*a), index(*b)) for a, b in pairs])

    def swap(x, by):
        a, b, c = by
        return send(x, [((i, j, k), (i ^ a, j ^ b, k ^ c)) for i, j, k in spots])

    def hop(x, source, target):
        return send(x, [((source, j, k), (target, j, k)) for i, j, k in spots if i == source])

    hbm = pltpu.HBM
    parcel = call(
        parcel_kernel,
        shape(BLK + 16),
        (members[0], edge_blocks, edge_shift),
        [hbm] * 3,
        [pltpu.VMEM((16, width), F32), pltpu.VMEM((16, slots), jnp.int32), pltpu.SemaphoreType.DMA((3,))],
    )
    arrived = [
        send(parcel, [((i, i ^ r, k), (0, i, k)) for i in range(layers) for k in range(cores)])
        for r in range(doms)
    ]

    own = (mats, biases[0], norm_gains[0])
    half = call(
        half_kernel,
        shape(2 * part + RIDERS),
        (place[1:2], *own),
        [smem] + [hbm] * 3,
        [pltpu.VMEM((4, width), F32), pltpu.SemaphoreType.DMA((3,))],
    )
    half = hop(half, layers - 1, SECOND)

    def handed(inputs, at, to):
        lead = hop(run_layers(place, at, inputs, slots, own, chosen=(0, 2)), at, to)
        rest = run_layers(place, at, inputs, slots, own, chosen=(2, 4))
        return lead, rest

    lead, rest = handed(arrived, 0, 1)
    state = [lead, hop(rest, 0, 1)]
    lead, rest = handed(state, 1, SECOND)
    half = lax.optimization_barrier((half, rest))[0]
    given = (half, swap(half, (0, 0, 1)))
    state = [lead, hop(rest, 1, SECOND)]
    blocks = run_layers(place, SECOND, state, slots, own, given, split=True)

    columns = [blocks[0]] + [swap(blocks[r], (0, r, 0)) for r in range(1, doms)]
    targets = [i for i in range(layers) if i != SECOND] + [SECOND]
    packed = call(
        messages_kernel,
        [shape(2 * BLK)] * layers,
        (place, *columns),
        [smem] + [vmem] * doms,
        [pltpu.VMEM((doms, BLK, width), BF16)],
        targets=targets,
    )
    final = packed[-1]
    for i, message in zip(targets[:-1], packed):
        final = jnp.where(s == i, hop(message, SECOND, i), final)
    total = final[BLK:]
    total = total.astype(F32) + swap(total, (0, 0, 1)).astype(F32)
    count = members.shape[0] * layers * cores
    return (final[None, :BLK], total / count)


def solution(mesh):
    shape = dict(mesh.shape)
    placed = (
        P(("section", "ens"), "dom", None),
        P("section", None, None, None),
        P("section", None, None),
        P("section", None, None),
        P("dom", None),
        P("dom", None),
    )

    def on_device(members, layer_mats, biases, norm_gains, edge_blocks, edge_shift):
        small = shape["section"] == 4 and shape["dom"] == 4 and shape["ens"] == 2
        one_each = members.shape[:2] == (1, BLK) and layer_mats.shape[0] == 1
        plan = in_two_stages if small and one_each else in_rounds
        return plan(members, layer_mats, biases, norm_gains, edge_blocks, edge_shift)

    return jax.shard_map(
        on_device,
        mesh=mesh,
        in_specs=placed,
        out_specs=(P(("section", "ens"), "dom", None), P("dom", None)),
        check_vma=False,
    )
```
